32 devices in a mesh: grid: 2 (over x), row: 4 (over y, core), col: 4 (over z).
Axes of the slice: x: 2, y: 2, z: 4, core: 2. Of those that a mesh axis runs over, the one named last changes fastest.
Arguments:
- rhs_in: bfloat16 [32768, 1024], P(('grid', 'row', 'col')), may hold values from -6 to 6
- rhs_target: int32 [32768], P(('grid', 'row', 'col')), may hold values from 0 to 32767, as said below
- leaf_inverse: bfloat16 [64, 512, 512], P(('grid', 'row', 'col')), may hold values from -0.25 to 0.25
- level_one_blocks: bfloat16 [2, 4, 4, 4, 2, 512, 512], P('grid', 'row', 'col'), may hold values from -0.0625 to 0.0625
- level_one_pattern: int32 [2, 4, 4, 4, 2], P('grid', 'row', 'col'), may hold values 0 or 1
- level_one_rhs: bfloat16 [2, 4, 512, 1024], P('grid', 'row', None, 'col'), may hold values from -6 to 6
- level_one_inverse: bfloat16 [2, 4, 512, 512], P('grid', 'row'), may hold values from -0.25 to 0.25
- top_blocks: bfloat16 [2, 4, 4, 512, 512], P('grid', 'row'), may hold values from -0.09375 to 0.09375
- top_rhs: bfloat16 [4, 512, 1024], P(None, None, 'col'), may hold values from -6 to 6
- top_inverse: bfloat16 [4, 512, 512], replicated, may hold values from -0.25 to 0.25
- top_chain: bfloat16 [6, 512, 512], replicated, may hold values from -0.125 to 0.125
Outputs:
- leaf_solution: bfloat16 [32768, 1024], P(('grid', 'row', 'col'))
- level_one_solution: bfloat16 [2, 4, 512, 1024], P('grid', 'row', None, 'col')
- top_solution: bfloat16 [4, 512, 1024], P(None, None, 'col')
The draws below stay inside these ranges and needn't reach their ends.
Inputs may be any that keep to these rules, and one draw needn't show every extreme that they name: rhs_target is a permutation; position p belongs to the device of flat index p // 1024 over grid, row, col (grid slowest); the 1024 arrival rows of every device go exactly 32 to each device.
All inputs are finite; a program needn't handle non-finite values. No bound on the sum of `level_one_pattern` on one device may be relied on, other than what follows from the above.
Results may differ from the reference program's by a relative error of at most 0.02.
Values may be sent and summed in bfloat16 or wider, within the bound.
A program may use at most 128 MiB of HBM per device.

```python
import jax
import jax.numpy as jnp
from jax import lax

S = 512
R = 1024
LEAF_DEV = 2
TOPS = 4
GRIDS = 2
BROWS = 4
BCOLS = 4
ROWS_DEV = 1024
ALL_ROWS = 32768
LEAVES = 64
PAIRS = 6


def draw_rhs_target(key, part):
    device_count = ALL_ROWS // ROWS_DEV
    share_rows = ROWS_DEV // device_count
    first_key, second_key = jax.random.split(jax.random.fold_in(key, 17))
    column_ids = jnp.arange(ROWS_DEV, dtype=jnp.int32)[None, :]
    scores = jax.random.randint(first_key, (device_count, ROWS_DEV), 0, 65536) * ROWS_DEV + column_ids
    local_order = jnp.argsort(scores, axis=1).astype(jnp.int32)
    grouped = local_order.reshape(device_count, device_count, share_rows)
    owners = jnp.arange(device_count, dtype=jnp.int32)[:, None, None] * ROWS_DEV
    positions = grouped + owners
    per_source = jnp.transpose(positions, (1, 0, 2)).reshape(device_count, ROWS_DEV)
    shuffle_scores = jax.random.randint(second_key, (device_count, ROWS_DEV), 0, 65536) * ROWS_DEV + column_ids
    shuffle = jnp.argsort(shuffle_scores, axis=1)
    mixed = jnp.take_along_axis(per_source, shuffle, axis=1)
    return mixed.reshape(ALL_ROWS).astype(jnp.int32)


def set_ends(array, rng, low, high):
    place = [jax.random.randint(jax.random.fold_in(rng, axis), (), 0, length) for axis, length in enumerate(array.shape)]
    main_axis = array.shape.index(max(array.shape))
    next_to = place[:main_axis] + [(place[main_axis] + 1) % array.shape[main_axis]] + place[main_axis + 1:]
    return array.at[tuple(place)].set(low).at[tuple(next_to)].set(high)


def block_levels(own_key, extent, cuts, least, top_value):
    def one(axis_at, shards_of):
        steps = jax.random.uniform(jax.random.fold_in(jax.random.fold_in(own_key, 6), axis_at), (shards_of,), jnp.float32, least / len(cuts), top_value / len(cuts))
        return jnp.repeat(jnp.exp(steps), extent[axis_at] // shards_of).reshape((-1,) + (1,) * (len(extent) - axis_at - 1))

    level = one(*cuts[0])
    for cut in cuts[1:]:
        level = level * one(*cut)
    return level


def bell_draw(stream_key, extent, scale, limit, cuts=(), held_as=jnp.bfloat16):
    factor_of = block_levels(stream_key, extent, cuts, -0.22, 0.18) if cuts else 1.0
    array = jax.random.normal(stream_key, extent, jnp.float32) * scale * factor_of
    return jnp.minimum(jnp.maximum(array, -limit), limit).astype(held_as)


def setup_inputs(seed: int = 0) -> dict:
    splits = jax.random.split(jax.random.key(seed), 12)
    rhs_in = bell_draw(splits[0], (ALL_ROWS, R), 1.0, 6.0, ((0, 32),))
    rhs_target = draw_rhs_target(jax.random.fold_in(splits[11], 71), 0)
    leaf_inverse = bell_draw(splits[2], (LEAVES, S, S), S ** -0.5, 0.25, ((0, 32),))
    level_one_blocks = bell_draw(splits[3], (GRIDS, BROWS, BCOLS, BROWS, LEAF_DEV, S, S), (BROWS * BCOLS * LEAF_DEV * S // 2) ** -0.5, 0.0625, ((0, 2), (1, 4), (2, 4)))
    level_one_pattern = set_ends((jax.random.randint(splits[4], (GRIDS, BROWS, BCOLS, BROWS, LEAF_DEV), 0, 2) < 1).astype(jnp.int32), jax.random.fold_in(splits[4], 1), 0, 1)
    level_one_rhs = bell_draw(splits[5], (GRIDS, BROWS, S, R), 1.0, 6.0, ((0, 2), (1, 4), (3, 4)))
    level_one_inverse = bell_draw(splits[6], (GRIDS, BROWS, S, S), S ** -0.5, 0.25, ((0, 2), (1, 4)))
    top_blocks = bell_draw(splits[7], (GRIDS, BROWS, TOPS, S, S), (GRIDS * BROWS * S) ** -0.5, 0.09375, ((0, 2), (1, 4)))
    top_rhs = bell_draw(splits[8], (TOPS, S, R), 1.0, 6.0, ((2, 4),))
    top_inverse = bell_draw(splits[9], (TOPS, S, S), S ** -0.5, 0.25)
    top_chain = bell_draw(splits[10], (PAIRS, S, S), (TOPS * S) ** -0.5, 0.125)
    return {"rhs_in": rhs_in, "rhs_target": rhs_target, "leaf_inverse": leaf_inverse, "level_one_blocks": level_one_blocks, "level_one_pattern": level_one_pattern, "level_one_rhs": level_one_rhs, "level_one_inverse": level_one_inverse, "top_blocks": top_blocks, "top_rhs": top_rhs, "top_inverse": top_inverse, "top_chain": top_chain}


def leaf_solve(operands):
    inverse_block, rhs_block = operands
    return jnp.dot(inverse_block, rhs_block, preferred_element_type=jnp.float32).astype(jnp.bfloat16)


def level_one_grid(operands):
    leaf_grid, blocks, pattern, rhs_one, inverse_one = operands
    solved = leaf_grid.astype(jnp.float32)
    masked = blocks.astype(jnp.float32) * pattern.astype(jnp.float32)[..., None, None]
    update_one = jnp.einsum("kcmlij,mcljr->kir", masked, solved)
    resid_one = (rhs_one.astype(jnp.float32) - update_one).astype(jnp.bfloat16)
    return jnp.einsum("kij,kjr->kir", inverse_one.astype(jnp.float32), resid_one.astype(jnp.float32)).astype(jnp.bfloat16)


def reference(rhs_in, rhs_target, leaf_inverse, level_one_blocks, level_one_pattern, level_one_rhs, level_one_inverse, top_blocks, top_rhs, top_inverse, top_chain):
    placed = rhs_in[jnp.argsort(rhs_target)]
    leaf_rhs = placed.reshape(LEAVES, S, R)
    leaf_solution = lax.map(leaf_solve, (leaf_inverse, leaf_rhs))
    leaf_grid = leaf_solution.reshape(GRIDS, BROWS, BCOLS, LEAF_DEV, S, R)
    level_one_solution = lax.map(level_one_grid, (leaf_grid, level_one_blocks, level_one_pattern, level_one_rhs, level_one_inverse))
    top_update = jnp.einsum("gktij,gkjr->tir", top_blocks.astype(jnp.float32), level_one_solution.astype(jnp.float32))
    solved = []
    for current in range(TOPS):
        running = top_rhs[current].astype(jnp.float32) - top_update[current]
        for earlier in range(current):
            running = running - jnp.dot(top_chain[current * (current - 1) // 2 + earlier], solved[earlier], preferred_element_type=jnp.float32)
        solved.append(jnp.dot(top_inverse[current], running.astype(jnp.bfloat16), preferred_element_type=jnp.float32).astype(jnp.bfloat16))
    top_solution = jnp.stack(solved)
    return leaf_solution.reshape(ALL_ROWS, R), level_one_solution, top_solution
```

```python
import functools

import jax
import jax.numpy as jnp
from jax import lax
from jax.experimental import pallas as pl
from jax.experimental.pallas import tpu as pltpu
from jax.sharding import PartitionSpec as P

MESH = pl.DeviceIdType.MESH
ANY = pl.BlockSpec(memory_space=pl.ANY)


def greet(axes, sizes):
    barrier = pltpu.get_barrier_semaphore()
    total = 1
    for size in sizes:
        total *= size
    flat = 0
    for axis, size in zip(axes, sizes):
        flat = flat * size + lax.axis_index(axis)

    @pl.loop(1, total)
    def _(step):
        rest = lax.rem(flat + step, total)
        coords = {}
        for axis, size in reversed(list(zip(axes, sizes))):
            coords[axis] = lax.rem(rest, size)
            rest = rest // size
        pl.semaphore_signal(barrier, inc=1, device_id=coords, device_id_type=MESH)

    return lambda: pl.semaphore_wait(barrier, total - 1)


def dot(a, b):
    return jnp.dot(a, b, preferred_element_type=jnp.float32)


def dot_t(a, b):
    return lax.dot_general(a, b, (((1,), (1,)), ((), ())), preferred_element_type=jnp.float32)


def lower_kernel(
    sizes,
    order,
    target_hbm,
    rhs_hbm,
    inverse_hbm,
    blocks_hbm,
    pattern_ref,
    rhs_one_hbm,
    inverse_one_hbm,
    top_rhs_hbm,
    top_blocks_hbm,
    top_inverse_hbm,
    chain_hbm,
    leaf_hbm,
    one_hbm,
    top_hbm,
    targets,
    rhs,
    inverse,
    own_blocks,
    rhs_one,
    inverse_one,
    top_rhs,
    top_blocks,
    top_inverse,
    chain,
    perm,
    fold,
    sorted_rows,
    got,
    places_out,
    got_places,
    other_blocks,
    solved,
    gathered,
    totals,
    pieces,
    landed,
    rhs_turned,
    terms,
    mate_terms,
    summed,
    sums,
    stacked,
    leaf,
    one,
    top_out,
    load_sems,
    leaf_sems,
    result_sems,
    block_sems,
    place_sems,
    row_send,
    row_recv,
    gather_send,
    gather_recv,
    piece_send,
    piece_recv,
    mate_send,
    mate_recv,
    sum_send,
    sum_recv,
    out_send,
    out_recv,
    on_send,
    on_recv,
):
    grids, rows, cols = sizes
    devices = grids * rows * cols
    row = lax.axis_index("row")
    col = lax.axis_index("col")
    me = (lax.axis_index("grid") * rows + row) * cols + col
    side = lax.rem(row, 2)
    mate = row + 1 - 2 * side
    leaves, size, _ = inverse.shape
    height = leaves * size
    chunk = leaf.shape[1] // cols
    half = chunk // 2
    share = got.shape[2]
    group = 128 // share

    met = greet(("grid", "row", "col"), sizes)
    loads = [
        pltpu.make_async_copy(source, into, load_sems.at[at])
        for at, (source, into) in enumerate(
            (
                (target_hbm, targets),
                (rhs_hbm, rhs),
                (inverse_hbm, inverse),
                (blocks_hbm, own_blocks),
                (rhs_one_hbm, rhs_one),
                (inverse_one_hbm, inverse_one),
                (top_rhs_hbm, top_rhs),
                (top_blocks_hbm, top_blocks),
                (top_inverse_hbm, top_inverse),
                (chain_hbm, chain),
            )
        )
    ]
    for load in loads:
        load.start()

    def column_of(part, which):
        pair = order[part // 2 * 2 : part // 2 * 2 + 2]
        return pair[which] if part % 2 == 0 else pair[1 - which]

    def columns(part, which):
        begin = column_of(part, which) * chunk + part % 2 * half
        return slice(begin, begin + half)

    def row_at(offset):
        pair = lax.rem(row // 2 + offset // 2, rows // 2)
        return pair * 2 + lax.rem(side + offset % 2, 2)

    def device_of(flat):
        return {
            "grid": flat // (rows * cols),
            "row": lax.rem(flat // cols, rows),
            "col": lax.rem(flat, cols),
        }

    def drain(ref, sem):
        pltpu.make_async_copy(ref, ref, sem).wait()

    def peer(step):
        return lax.rem(me + step, devices)

    def place_copy(step):
        target = peer(step)
        return pltpu.make_async_remote_copy(
            src_ref=places_out.at[target],
            dst_ref=got_places.at[me],
            send_sem=place_sems.at[0],
            recv_sem=place_sems.at[1],
            device_id=device_of(target),
            device_id_type=MESH,
        )

    def row_copy(part, step):
        target = peer(step)
        return pltpu.make_async_remote_copy(
            src_ref=sorted_rows.at[part, target],
            dst_ref=got.at[part, me],
            send_sem=row_send.at[part],
            recv_sem=row_recv.at[part],
            device_id=device_of(target),
            device_id_type=MESH,
        )

    block_copy = pltpu.make_async_remote_copy(
        src_ref=own_blocks,
        dst_ref=other_blocks,
        send_sem=block_sems.at[0],
        recv_sem=block_sems.at[1],
        device_id={"row": mate},
        device_id_type=MESH,
    )

    def gather_copy(part, target, owner):
        return pltpu.make_async_remote_copy(
            src_ref=solved.at[part, lax.rem(target, 2)],
            dst_ref=gathered.at[part, owner],
            send_sem=gather_send.at[part],
            recv_sem=gather_recv.at[part, owner],
            device_id={"row": target},
            device_id_type=MESH,
        )

    def piece_copy(part, which, into):
        return pltpu.make_async_remote_copy(
            src_ref=pieces.at[part, which],
            dst_ref=landed.at[part % 2, col],
            send_sem=piece_send.at[which],
            recv_sem=piece_recv.at[part % 2],
            device_id={"row": mate if which else row, "col": into},
            device_id_type=MESH,
        )

    span = height
    before = lax.broadcasted_iota(jnp.int32, (span, span), 0)
    after = lax.broadcasted_iota(jnp.int32, (span, span), 1)
    perm[...] = jnp.where(before < after, 1.0, 0.0).astype(perm.dtype)
    loads[0].wait()
    destination = targets[...] // height
    place = lax.rem(targets[...], height)
    for_device = lax.broadcasted_iota(jnp.int32, (devices, height), 0) == destination
    ones = jnp.where(for_device, 1.0, 0.0)
    counted = dot(ones.astype(perm.dtype), perm[...])
    rank = jnp.sum(ones * counted, axis=0, keepdims=True).astype(jnp.int32)
    slot = destination * share + rank

    step_rows = 256
    for begin in range(0, height, step_rows):
        index = lax.broadcasted_iota(jnp.int32, (step_rows, height), 0) + begin
        perm[begin : begin + step_rows, :] = (
            jnp.where(index == slot, 1.0, 0.0).astype(perm.dtype)
        )
    loads[1].wait()

    def send_rows(part):
        @pl.loop(1, devices)
        def _(step):
            row_copy(part, step).start()

    for part in range(cols):
        taken = jnp.concatenate([rhs[:, columns(part, which)] for which in range(2)], axis=1)
        moved = dot(perm[...], taken).astype(got.dtype)
        sorted_rows[part] = moved.reshape(devices, share, chunk)
        if part == 0:
            met()
        if part < 2:
            send_rows(part)
        got[part, me] = sorted_rows[part, me]
        if part == 0:
            lane = lax.broadcasted_iota(jnp.int32, (128, height), 0)
            to_lane = jnp.where(lane == lax.rem(me, group) * share + rank, 1.0, 0.0)
            to_lane = to_lane.astype(perm.dtype)
            high = (ones * (place // 32).astype(jnp.float32)).astype(perm.dtype)
            low = (ones * lax.rem(place, 32).astype(jnp.float32)).astype(perm.dtype)
            spread = dot_t(high, to_lane) * 32.0 + dot_t(low, to_lane)
            places_out[...] = spread.astype(jnp.int32).reshape(devices, 1, 128)

            @pl.loop(1, devices)
            def _(step):
                place_copy(step).start()

            got_places[me] = places_out[me]

    def masked(block, scale):
        return (block.astype(jnp.float32) * scale).astype(block.dtype)

    loads[3].wait()

    @pl.loop(0, rows)
    def _(owner):
        for leaf_at in range(leaves):
            own_blocks[owner, leaf_at] = masked(
                own_blocks[owner, leaf_at], pattern_ref[owner, leaf_at].astype(jnp.float32)
            )

    block_copy.start()
    loads[2].wait()
    drain(got_places.at[pl.ds(0, devices - 1)], place_sems.at[1])

    for block in range(height // 128):
        places = got_places[block * group]
        for other in range(1, group):
            places = places + got_places[block * group + other]
        index = lax.broadcasted_iota(jnp.int32, (height, 128), 0)
        perm[:, block * 128 : (block + 1) * 128] = jnp.where(index == places, 1.0, 0.0).astype(
            perm.dtype
        )
    for at in range(leaves):
        of_leaf = slice(at * size, (at + 1) * size)
        fold[of_leaf, :] = dot(inverse[at], perm[of_leaf, :]).astype(fold.dtype)

    for load in loads[4:]:
        load.wait()

    tops = top_blocks.shape[0]
    pairs = grids * rows // 2
    depth = terms.shape[3]
    for top in range(tops):
        rhs_turned[top] = top_rhs[top].T.reshape(2 * pairs, depth, size)

    def leaf_copy(part, which):
        return pltpu.make_async_copy(
            leaf.at[:, columns(part, which)], leaf_hbm.at[:, columns(part, which)], leaf_sems.at[part, which]
        )

    def solve(part):
        drain(got.at[part, pl.ds(0, devices - 1)], row_recv.at[part])
        result = dot(fold[...], got[part].reshape(height, chunk)).astype(leaf.dtype)
        for which in range(2):
            solved[part, which] = result[:, which * half : (which + 1) * half]
        for offset in range(rows - 1, 0, -1):
            gather_copy(part, row_at(offset), row).start()
        gathered[part, row] = solved[part, side]
        for which in range(2):
            leaf[:, columns(part, which)] = result[:, which * half : (which + 1) * half]
            leaf_copy(part, which).start()

    def add(part, owner):
        for which, blocks in enumerate((own_blocks, other_blocks)):
            term = dot(blocks[owner, 0], gathered[part, owner, :size])
            for at in range(1, leaves):
                term = term + dot(
                    blocks[owner, at], gathered[part, owner, at * size : (at + 1) * size]
                )
            totals[which] += term

    def couple(part):
        totals[...] = jnp.zeros_like(totals)

        @pl.loop(0, rows)
        def _(offset):
            owner = row_at(offset)

            @pl.when(offset > 0)
            def _():
                gather_copy(part, owner, owner).wait_recv()

            add(part, owner)

        into = column_of(part, 0) + side * (column_of(part, 1) - column_of(part, 0))
        pieces[part] = totals[...].astype(pieces.dtype)
        piece_copy(part, 1, into).start()

        @pl.when(col != into)
        def _():
            piece_copy(part, 0, into).start()

        @pl.when(col == into)
        def _():
            landed[part % 2, col] = pieces[part, 0]

    for part in range(cols):
        solve(part)
        if part + 2 < cols:
            send_rows(part + 2)
        if part == 0:
            block_copy.wait()
        else:
            couple(part - 1)
    couple(cols - 1)

    second = 0
    for at in range(1, cols, 2):
        second = second + jnp.where(col == order[at], 1, 0)
    near = side + second - 2 * side * second
    drain(landed.at[near, pl.ds(0, cols - 1)], piece_recv.at[near])
    drain(landed.at[1 - near], piece_recv.at[1 - near])
    update = []
    for which in range(2):
        total = landed[which, 0].astype(jnp.float32)
        for source in range(1, cols):
            total = total + landed[which, source].astype(jnp.float32)
        update.append(total)
    resid = rhs_one[...].astype(jnp.float32) - jnp.concatenate(update, axis=1)
    solution_one = dot(inverse_one[...], resid.astype(jnp.bfloat16)).astype(one.dtype)

    pair = (lax.axis_index("grid") * rows + row) // 2
    here = 2 * pair + side

    def pair_at(step):
        return lax.rem(pair + step, pairs)

    def across(target):
        return {
            "grid": target // (rows // 2),
            "row": lax.rem(target, rows // 2) * 2 + side,
        }

    def mate_copy(top):
        return pltpu.make_async_remote_copy(
            src_ref=terms.at[top, 1 - side],
            dst_ref=mate_terms.at[top],
            send_sem=mate_send.at[top],
            recv_sem=mate_recv.at[top],
            device_id={"row": mate},
            device_id_type=MESH,
        )

    def sum_copy(top, target):
        return pltpu.make_async_remote_copy(
            src_ref=summed.at[top, target],
            dst_ref=sums.at[top, pair],
            send_sem=sum_send,
            recv_sem=sum_recv.at[top],
            device_id=across(target),
            device_id_type=MESH,
        )

    def out_copy(top, target, source):
        return pltpu.make_async_remote_copy(
            src_ref=stacked.at[top, here],
            dst_ref=stacked.at[top, 2 * source + side],
            send_sem=out_send,
            recv_sem=out_recv.at[top, source],
            device_id=across(target),
            device_id_type=MESH,
        )

    def on_copy(top, source):
        return pltpu.make_async_remote_copy(
            src_ref=stacked.at[top, 2 * source + side],
            dst_ref=stacked.at[top, 2 * source + side],
            send_sem=on_send,
            recv_sem=on_recv.at[top],
            device_id={"row": mate},
            device_id_type=MESH,
        )

    turned = solution_one.T
    for top in range(tops):
        term = dot_t(turned, top_blocks[top])
        for target in range(2 * pairs):
            terms[top, target % 2, target // 2] = term[
                target * depth : (target + 1) * depth
            ].astype(terms.dtype)
        mate_copy(top).start()
    one[...] = solution_one
    one_copy = pltpu.make_async_copy(one, one_hbm, result_sems.at[tops])
    one_copy.start()
    for top in range(tops):
        mate_copy(top).wait_recv()
        summed[top] = (
            terms[top, side].astype(jnp.float32) + mate_terms[top].astype(jnp.float32)
        ).astype(summed.dtype)
        for step in range(1, pairs):
            sum_copy(top, pair_at(step)).start()
    for top in range(tops):
        sums[top, pair] = summed[top, pair]
        drain(sums.at[top, pl.ds(0, pairs - 1)], sum_recv.at[top])
        update = sums[top, 0].astype(jnp.float32)
        for other in range(1, pairs):
            update = update + sums[top, other].astype(jnp.float32)
        running = rhs_turned[top, here].astype(jnp.float32) - update
        for earlier in range(top):
            running = running - dot_t(
                stacked[earlier, here], chain[top * (top - 1) // 2 + earlier]
            )
        stacked[top, here] = dot_t(running.astype(jnp.bfloat16), top_inverse[top]).astype(
            stacked.dtype
        )
        for step in range(1, pairs):
            out_copy(top, pair_at(step), pair).start()
        on_copy(top, pair).start()
    top_copies = [
        pltpu.make_async_copy(top_out.at[top], top_hbm.at[top], result_sems.at[top])
        for top in range(tops)
    ]
    for top in range(tops):
        for step in range(1, pairs):
            source = pair_at(step)
            out_copy(top, source, source).wait_recv()
            on_copy(top, source).start()
        drain(stacked.at[top, pl.ds(0, pairs)], on_recv.at[top])
        top_out[top] = stacked[top].reshape(2 * pairs * depth, size).T
        top_copies[top].start()

    drain(places_out.at[pl.ds(0, devices - 1)], place_sems.at[0])
    drain(pieces.at[:, 1], piece_send.at[1])

    for part in range(cols):
        drain(sorted_rows.at[part, pl.ds(0, devices - 1)], row_send.at[part])
        drain(gathered.at[part, pl.ds(0, rows - 1)], gather_send.at[part])
        for which in range(2):
            leaf_copy(part, which).wait()
    drain(pieces.at[pl.ds(0, cols - 1), 0], piece_send.at[0])
    for top in range(tops):
        mate_copy(top).wait_send()
        top_copies[top].wait()
    drain(summed.at[:, pl.ds(0, pairs - 1)], sum_send)
    drain(stacked.at[:, pl.ds(0, pairs - 1)], out_send)
    drain(stacked.at[:, pl.ds(0, pairs)], on_send)
    one_copy.wait()


def all_levels(rhs_in, target, leaf_inverse, blocks, pattern, rhs, inverse, top_blocks, top_rhs, *rest):
    sizes = tuple(lax.axis_size(axis) for axis in ("grid", "row", "col"))
    grids, rows, cols = sizes
    devices = grids * rows * cols
    height, width = rhs_in.shape
    share = height // devices
    owners, leaves, size, _ = blocks.shape
    chunk = width // cols
    half = chunk // 2
    bf16 = jnp.bfloat16
    order = sorted(range(cols), key=lambda part: -abs(2 * part - (cols - 1)))

    dma = pltpu.SemaphoreType.DMA
    tops = top_blocks.shape[0]
    pairs = grids * rows // 2
    depth = chunk // (2 * pairs)
    held = (rhs_in, leaf_inverse, blocks, rhs, inverse, top_rhs, top_blocks, *rest)
    smem = pl.BlockSpec(memory_space=pltpu.SMEM)
    return pl.pallas_call(
        functools.partial(lower_kernel, sizes, order),
        out_shape=(
            jax.ShapeDtypeStruct((height, width), bf16),
            jax.ShapeDtypeStruct(rhs.shape, bf16),
            jax.ShapeDtypeStruct(top_rhs.shape, bf16),
        ),
        in_specs=[ANY, ANY, ANY, ANY, smem, *(ANY for _ in range(6))],
        out_specs=(ANY, ANY, ANY),
        scratch_shapes=[
            pltpu.VMEM((1, height), jnp.int32),
            *(pltpu.VMEM(array.shape, bf16) for array in held),
            pltpu.VMEM((height, height), bf16),
            pltpu.VMEM((height, height), bf16),
            pltpu.VMEM((cols, devices, share, chunk), bf16),
            pltpu.VMEM((cols, devices, share, chunk), bf16),
            pltpu.VMEM((devices, 1, 128), jnp.int32),
            pltpu.VMEM((devices, 1, 128), jnp.int32),
            pltpu.VMEM(blocks.shape, bf16),
            pltpu.VMEM((cols, 2, height, half), bf16),
            pltpu.VMEM((cols, rows, height, half), bf16),
            pltpu.VMEM((2, size, half), jnp.float32),
            pltpu.VMEM((cols, 2, size, half), bf16),
            pltpu.VMEM((2, cols, size, half), bf16),
            pltpu.VMEM((tops, 2 * pairs, depth, size), bf16),
            pltpu.VMEM((tops, 2, pairs, depth, size), bf16),
            pltpu.VMEM((tops, pairs, depth, size), bf16),
            pltpu.VMEM((tops, pairs, depth, size), bf16),
            pltpu.VMEM((tops, pairs, depth, size), bf16),
            pltpu.VMEM((tops, 2 * pairs, depth, size), bf16),
            pltpu.VMEM((height, width), bf16),
            pltpu.VMEM(rhs.shape, bf16),
            pltpu.VMEM(top_rhs.shape, bf16),
            dma((len(held) + 1,)),
            dma((cols, 2)),
            dma((tops + 1,)),
            dma((2,)),
            dma((2,)),
            dma((cols,)),
            dma((cols,)),
            dma((cols,)),
            dma((cols, rows)),
            dma((2,)),
            dma((2,)),
            dma((tops,)),
            dma((tops,)),
            dma,
            dma((tops,)),
            dma,
            dma((tops, pairs)),
            dma,
            dma((tops,)),
        ],
        compiler_params=pltpu.CompilerParams(
            collective_id=1, has_side_effects=True, vmem_limit_bytes=60 * 2**20
        ),
        name="lower",
    )(
        target[None, :], rhs_in, leaf_inverse, blocks, pattern, rhs, inverse, top_rhs, top_blocks, *rest
    )


def shards(
    rhs_in,
    rhs_target,
    leaf_inverse,
    level_one_blocks,
    level_one_pattern,
    level_one_rhs,
    level_one_inverse,
    top_blocks,
    top_rhs,
    top_inverse,
    top_chain,
):
    leaf_solution, solution_one, top_solution = all_levels(
        rhs_in,
        rhs_target,
        leaf_inverse,
        level_one_blocks[0, 0, 0],
        level_one_pattern[0, 0, 0],
        level_one_rhs[0, 0],
        level_one_inverse[0, 0],
        top_blocks[0, 0],
        top_rhs,
        top_inverse,
        top_chain,
    )
    return (leaf_solution, solution_one[None, None], top_solution)


def solution(mesh):
    in_specs = (
        P(("grid", "row", "col"), None),
        P(("grid", "row", "col")),
        P(("grid", "row", "col"), None, None),
        P("grid", "row", "col", None, None, None, None),
        P("grid", "row", "col", None, None),
        P("grid", "row", None, "col"),
        P("grid", "row", None, None),
        P("grid", "row", None, None, None),
        P(None, None, "col"),
        P(),
        P(),
    )
    out_specs = (
        P(("grid", "row", "col"), None),
        P("grid", "row", None, "col"),
        P(None, None, "col"),
    )
    return jax.shard_map(shards, mesh=mesh, in_specs=in_specs, out_specs=out_specs, check_vma=False)
```

```python
import functools

import jax
import jax.numpy as jnp
from jax import lax
from jax.experimental import pallas as pl
from jax.experimental.pallas import tpu as pltpu
from jax.sharding import PartitionSpec as P

MESH = pl.DeviceIdType.MESH
ANY = pl.BlockSpec(memory_space=pl.ANY)


def greet(axes, sizes):
    barrier = pltpu.get_barrier_semaphore()
    total = 1
    for size in sizes:
        total *= size
    flat = 0
    for axis, size in zip(axes, sizes):
        flat = flat * size + lax.axis_index(axis)

    @pl.loop(1, total)
    def _(step):
        rest = lax.rem(flat + step, total)
        coords = {}
        for axis, size in reversed(list(zip(axes, sizes))):
            coords[axis] = lax.rem(rest, size)
            rest = rest // size
        pl.semaphore_signal(barrier, inc=1, device_id=coords, device_id_type=MESH)

    return lambda: pl.semaphore_wait(barrier, total - 1)


def dot(a, b):
    return jnp.dot(a, b, preferred_element_type=jnp.float32)


def dot_t(a, b):
    return lax.dot_general(a, b, (((1,), (1,)), ((), ())), preferred_element_type=jnp.float32)


STRIPS = 8


def hand_on(leaf_in, one_in, top_in, leaf_out, one_out, top_out, leaf, one, top, sems):
    moves = []
    tall = leaf.shape[0] // STRIPS
    for strip in range(STRIPS):
        where = pl.ds(strip * tall, tall)
        moves.append((leaf_in.at[where], leaf.at[where], leaf_out.at[where]))
    moves += [(one_in, one, one_out), (top_in, top, top_out)]
    taken = [
        pltpu.make_async_copy(source, held, sems.at[0, at])
        for at, (source, held, _) in enumerate(moves)
    ]
    given = [
        pltpu.make_async_copy(held, into, sems.at[1, at])
        for at, (_, held, into) in enumerate(moves)
    ]
    for copy in taken:
        copy.start()
    for copy, after in zip(taken, given):
        copy.wait()
        after.start()
    for after in given:
        after.wait()


def lower_kernel(
    sizes,
    order,
    target_hbm,
    rhs_hbm,
    inverse_hbm,
    blocks_hbm,
    pattern_ref,
    rhs_one_hbm,
    inverse_one_hbm,
    top_rhs_hbm,
    top_blocks_hbm,
    top_inverse_hbm,
    chain_hbm,
    leaf_hbm,
    one_hbm,
    top_hbm,
    targets,
    rhs,
    inverse,
    own_blocks,
    rhs_one,
    inverse_one,
    top_rhs,
    top_blocks,
    top_inverse,
    chain,
    perm,
    fold,
    sorted_rows,
    got,
    places_out,
    got_places,
    other_blocks,
    solved,
    gathered,
    totals,
    pieces,
    landed,
    rhs_turned,
    terms,
    mate_terms,
    summed,
    sums,
    stacked,
    leaf,
    one,
    top_out,
    load_sems,
    leaf_sems,
    result_sems,
    block_sems,
    place_sems,
    row_send,
    row_recv,
    gather_send,
    gather_recv,
    piece_send,
    piece_recv,
    mate_send,
    mate_recv,
    sum_send,
    sum_recv,
    out_send,
    out_recv,
    on_send,
    on_recv,
):
    grids, rows, cols = sizes
    devices = grids * rows * cols
    row = lax.axis_index("row")
    col = lax.axis_index("col")
    me = (lax.axis_index("grid") * rows + row) * cols + col
    side = lax.rem(row, 2)
    mate = row + 1 - 2 * side
    leaves, size, _ = inverse.shape
    height = leaves * size
    chunk = leaf.shape[1] // cols
    half = chunk // 2
    share = got.shape[2]
    group = 128 // share

    units = 2 * cols
    ahead = 4
    met = greet(("grid", "row", "col"), sizes)
    loads = [
        pltpu.make_async_copy(source, into, load_sems.at[at])
        for at, (source, into) in enumerate(
            (
                (target_hbm, targets),
                (rhs_hbm, rhs),
                (inverse_hbm, inverse),
                (blocks_hbm, own_blocks),
                (rhs_one_hbm, rhs_one),
                (inverse_one_hbm, inverse_one),
                (top_rhs_hbm, top_rhs),
                (top_blocks_hbm, top_blocks),
                (top_inverse_hbm, top_inverse),
                (chain_hbm, chain),
            )
        )
    ]
    for load in loads:
        load.start()

    def column_of(part, which):
        pair = order[part // 2 * 2 : part // 2 * 2 + 2]
        return pair[which] if part % 2 == 0 else pair[1 - which]

    def columns(part, which):
        begin = column_of(part, which) * chunk + part % 2 * half
        return slice(begin, begin + half)

    def row_at(offset):
        pair = lax.rem(row // 2 + offset // 2, rows // 2)
        return pair * 2 + lax.rem(side + offset % 2, 2)

    def device_of(flat):
        return {
            "grid": flat // (rows * cols),
            "row": lax.rem(flat // cols, rows),
            "col": lax.rem(flat, cols),
        }

    def drain(ref, sem):
        pltpu.make_async_copy(ref, ref, sem).wait()

    def peer(step):
        return lax.rem(me + step, devices)

    def place_copy(step):
        target = peer(step)
        return pltpu.make_async_remote_copy(
            src_ref=places_out.at[target],
            dst_ref=got_places.at[me],
            send_sem=place_sems.at[0],
            recv_sem=place_sems.at[1],
            device_id=device_of(target),
            device_id_type=MESH,
        )

    def row_copy(unit, step):
        target = peer(step)
        return pltpu.make_async_remote_copy(
            src_ref=sorted_rows.at[unit, target],
            dst_ref=got.at[unit, me],
            send_sem=row_send.at[unit],
            recv_sem=row_recv.at[unit],
            device_id=device_of(target),
            device_id_type=MESH,
        )

    block_copy = pltpu.make_async_remote_copy(
        src_ref=own_blocks,
        dst_ref=other_blocks,
        send_sem=block_sems.at[0],
        recv_sem=block_sems.at[1],
        device_id={"row": mate},
        device_id_type=MESH,
    )

    def gather_copy(unit, target, owner):
        part = unit // 2
        return pltpu.make_async_remote_copy(
            src_ref=solved.at[unit],
            dst_ref=gathered.at[part, owner],
            send_sem=gather_send.at[part],
            recv_sem=gather_recv.at[part, owner],
            device_id={"row": target},
            device_id_type=MESH,
        )

    def piece_copy(part, which, into):
        return pltpu.make_async_remote_copy(
            src_ref=pieces.at[part, which],
            dst_ref=landed.at[part % 2, col],
            send_sem=piece_send.at[which],
            recv_sem=piece_recv.at[part % 2],
            device_id={"row": mate if which else row, "col": into},
            device_id_type=MESH,
        )

    span = height
    before = lax.broadcasted_iota(jnp.int32, (span, span), 0)
    after = lax.broadcasted_iota(jnp.int32, (span, span), 1)
    perm[...] = jnp.where(before < after, 1.0, 0.0).astype(perm.dtype)
    loads[0].wait()
    destination = targets[...] // height
    place = lax.rem(targets[...], height)
    for_device = lax.broadcasted_iota(jnp.int32, (devices, height), 0) == destination
    ones = jnp.where(for_device, 1.0, 0.0)
    counted = dot(ones.astype(perm.dtype), perm[...])
    rank = jnp.sum(ones * counted, axis=0, keepdims=True).astype(jnp.int32)
    slot = destination * share + rank

    lane = lax.broadcasted_iota(jnp.int32, (128, height), 0)
    to_lane = jnp.where(lane == lax.rem(me, group) * share + rank, 1.0, 0.0).astype(perm.dtype)
    high = (ones * (place // 32).astype(jnp.float32)).astype(perm.dtype)
    low = (ones * lax.rem(place, 32).astype(jnp.float32)).astype(perm.dtype)
    spread = dot_t(high, to_lane) * 32.0 + dot_t(low, to_lane)
    places_out[...] = spread.astype(jnp.int32).reshape(devices, 1, 128)
    got_places[me] = places_out[me]

    step_rows = 256
    for begin in range(0, height, step_rows):
        index = lax.broadcasted_iota(jnp.int32, (step_rows, height), 0) + begin
        perm[begin : begin + step_rows, :] = (
            jnp.where(index == slot, 1.0, 0.0).astype(perm.dtype)
        )
    loads[1].wait()

    def send_rows(unit):
        @pl.loop(1, devices)
        def _(step):
            row_copy(unit, step).start()

    for part in range(cols):
        taken = jnp.concatenate([rhs[:, columns(part, which)] for which in range(2)], axis=1)
        moved = dot(perm[...], taken).astype(got.dtype)
        for which in range(2):
            unit = 2 * part + which
            sorted_rows[unit] = moved[:, which * half : (which + 1) * half].reshape(
                devices, share, half
            )
            if unit == 0:
                met()

                @pl.loop(1, devices)
                def _(step):
                    place_copy(step).start()

            if unit < ahead:
                send_rows(unit)
            got[unit, me] = sorted_rows[unit, me]

    def masked(block, scale):
        return (block.astype(jnp.float32) * scale).astype(block.dtype)

    loads[3].wait()

    @pl.loop(0, rows)
    def _(owner):
        for leaf_at in range(leaves):
            own_blocks[owner, leaf_at] = masked(
                own_blocks[owner, leaf_at], pattern_ref[leaf_at, owner].astype(jnp.float32)
            )

    block_copy.start()
    loads[2].wait()
    drain(got_places.at[pl.ds(0, devices - 1)], place_sems.at[1])

    for block in range(height // 128):
        places = got_places[block * group]
        for other in range(1, group):
            places = places + got_places[block * group + other]
        index = lax.broadcasted_iota(jnp.int32, (height, 128), 0)
        perm[:, block * 128 : (block + 1) * 128] = jnp.where(index == places, 1.0, 0.0).astype(
            perm.dtype
        )
    for at in range(leaves):
        of_leaf = slice(at * size, (at + 1) * size)
        fold[of_leaf, :] = dot(inverse[at], perm[of_leaf, :]).astype(fold.dtype)

    for load in loads[4:]:
        load.wait()

    tops = top_blocks.shape[0]
    pairs = grids * rows // 2
    depth = terms.shape[3]
    for top in range(tops):
        rhs_turned[top] = top_rhs[top].T.reshape(2 * pairs, depth, size)

    def leaf_copy(unit):
        where = columns(unit // 2, unit % 2)
        return pltpu.make_async_copy(leaf.at[:, where], leaf_hbm.at[:, where], leaf_sems.at[unit])

    def solve(unit):
        part, which = unit // 2, unit % 2
        drain(got.at[unit, pl.ds(0, devices - 1)], row_recv.at[unit])
        result = dot(fold[...], got[unit].reshape(height, half)).astype(leaf.dtype)
        solved[unit] = result
        for offset in range(1, rows // 2):
            target = lax.rem(row // 2 + offset, rows // 2) * 2 + which
            gather_copy(unit, target, row).start()

        @pl.when(side != which)
        def _():
            gather_copy(unit, mate, row).start()

        @pl.when(side == which)
        def _():
            gathered[part, row] = solved[unit]

        leaf[:, columns(part, which)] = result
        leaf_copy(unit).start()
        if unit + ahead < units:
            send_rows(unit + ahead)

    def add(part, owner):
        for which, blocks in enumerate((own_blocks, other_blocks)):
            term = dot(blocks[owner, 0], gathered[part, owner, :size])
            for at in range(1, leaves):
                term = term + dot(
                    blocks[owner, at], gathered[part, owner, at * size : (at + 1) * size]
                )
            totals[which] += term

    def couple(part):
        totals[...] = jnp.zeros_like(totals)

        @pl.loop(0, rows)
        def _(offset):
            owner = row_at(offset)

            @pl.when(offset > 0)
            def _():
                gather_copy(2 * part, owner, owner).wait_recv()

            add(part, owner)

        into = column_of(part, 0) + side * (column_of(part, 1) - column_of(part, 0))
        pieces[part] = totals[...].astype(pieces.dtype)
        piece_copy(part, 1, into).start()

        @pl.when(col != into)
        def _():
            piece_copy(part, 0, into).start()

        @pl.when(col == into)
        def _():
            landed[part % 2, col] = pieces[part, 0]

    for unit in range(units):
        solve(unit)
        if unit == 1:
            block_copy.wait()
        elif unit > 1 and unit % 2 == 0:
            couple(unit // 2 - 1)
    couple(cols - 1)

    second = 0
    for at in range(1, cols, 2):
        second = second + jnp.where(col == order[at], 1, 0)
    near = side + second - 2 * side * second
    drain(landed.at[near, pl.ds(0, cols - 1)], piece_recv.at[near])
    drain(landed.at[1 - near], piece_recv.at[1 - near])
    update = []
    for which in range(2):
        total = landed[which, 0].astype(jnp.float32)
        for source in range(1, cols):
            total = total + landed[which, source].astype(jnp.float32)
        update.append(total)
    resid = rhs_one[...].astype(jnp.float32) - jnp.concatenate(update, axis=1)
    solution_one = dot(inverse_one[...], resid.astype(jnp.bfloat16)).astype(one.dtype)

    pair = (lax.axis_index("grid") * rows + row) // 2
    here = 2 * pair + side

    def pair_at(step):
        return lax.rem(pair + step, pairs)

    def across(target):
        return {
            "grid": target // (rows // 2),
            "row": lax.rem(target, rows // 2) * 2 + side,
        }

    def mate_copy(top):
        return pltpu.make_async_remote_copy(
            src_ref=terms.at[top, 1 - side],
            dst_ref=mate_terms.at[top],
            send_sem=mate_send.at[top],
            recv_sem=mate_recv.at[top],
            device_id={"row": mate},
            device_id_type=MESH,
        )

    def sum_copy(top, target):
        return pltpu.make_async_remote_copy(
            src_ref=summed.at[top, target],
            dst_ref=sums.at[top, pair],
            send_sem=sum_send,
            recv_sem=sum_recv.at[top],
            device_id=across(target),
            device_id_type=MESH,
        )

    def out_copy(top, target, source):
        return pltpu.make_async_remote_copy(
            src_ref=stacked.at[top, here],
            dst_ref=stacked.at[top, 2 * source + side],
            send_sem=out_send,
            recv_sem=out_recv.at[top, source],
            device_id=across(target),
            device_id_type=MESH,
        )

    def on_copy(top, source):
        return pltpu.make_async_remote_copy(
            src_ref=stacked.at[top, 2 * source + side],
            dst_ref=stacked.at[top, 2 * source + side],
            send_sem=on_send,
            recv_sem=on_recv.at[top],
            device_id={"row": mate},
            device_id_type=MESH,
        )

    turned = solution_one.T
    for top in range(tops):
        term = dot_t(turned, top_blocks[top])
        for target in range(2 * pairs):
            terms[top, target % 2, target // 2] = term[
                target * depth : (target + 1) * depth
            ].astype(terms.dtype)
        mate_copy(top).start()
    one[...] = solution_one
    one_copy = pltpu.make_async_copy(one, one_hbm, result_sems.at[tops])
    one_copy.start()
    for top in range(tops):
        mate_copy(top).wait_recv()
        summed[top] = (
            terms[top, side].astype(jnp.float32) + mate_terms[top].astype(jnp.float32)
        ).astype(summed.dtype)
        for step in range(1, pairs):
            sum_copy(top, pair_at(step)).start()
    for top in range(tops):
        sums[top, pair] = summed[top, pair]
        drain(sums.at[top, pl.ds(0, pairs - 1)], sum_recv.at[top])
        update = sums[top, 0].astype(jnp.float32)
        for other in range(1, pairs):
            update = update + sums[top, other].astype(jnp.float32)
        running = rhs_turned[top, here].astype(jnp.float32) - update
        for earlier in range(top):
            running = running - dot_t(
                stacked[earlier, here], chain[top * (top - 1) // 2 + earlier]
            )
        stacked[top, here] = dot_t(running.astype(jnp.bfloat16), top_inverse[top]).astype(
            stacked.dtype
        )
        for step in range(1, pairs):
            out_copy(top, pair_at(step), pair).start()
        on_copy(top, pair).start()
    top_copies = [
        pltpu.make_async_copy(top_out.at[top], top_hbm.at[top], result_sems.at[top])
        for top in range(tops)
    ]
    for top in range(tops):
        for step in range(1, pairs):
            source = pair_at(step)
            out_copy(top, source, source).wait_recv()
            on_copy(top, source).start()
        drain(stacked.at[top, pl.ds(0, pairs)], on_recv.at[top])
        top_out[top] = stacked[top].reshape(2 * pairs * depth, size).T
        top_copies[top].start()

    drain(places_out.at[pl.ds(0, devices - 1)], place_sems.at[0])
    drain(pieces.at[:, 1], piece_send.at[1])

    for unit in range(units):
        drain(sorted_rows.at[unit, pl.ds(0, devices - 1)], row_send.at[unit])
        leaf_copy(unit).wait()
    for part in range(cols):
        drain(gathered.at[part, pl.ds(0, rows - 1)], gather_send.at[part])
    drain(pieces.at[pl.ds(0, cols - 1), 0], piece_send.at[0])
    for top in range(tops):
        mate_copy(top).wait_send()
        top_copies[top].wait()
    drain(summed.at[:, pl.ds(0, pairs - 1)], sum_send)
    drain(stacked.at[:, pl.ds(0, pairs - 1)], out_send)
    drain(stacked.at[:, pl.ds(0, pairs)], on_send)
    one_copy.wait()


def all_levels(rhs_in, target, leaf_inverse, blocks, pattern, rhs, inverse, top_blocks, top_rhs, *rest):
    sizes = tuple(lax.axis_size(axis) for axis in ("grid", "row", "col"))
    grids, rows, cols = sizes
    devices = grids * rows * cols
    height, width = rhs_in.shape
    share = height // devices
    owners, leaves, size, _ = blocks.shape
    chunk = width // cols
    half = chunk // 2
    bf16 = jnp.bfloat16
    order = sorted(range(cols), key=lambda part: -abs(2 * part - (cols - 1)))

    dma = pltpu.SemaphoreType.DMA
    tops = top_blocks.shape[0]
    pairs = grids * rows // 2
    depth = chunk // (2 * pairs)
    held = (rhs_in, leaf_inverse, blocks, rhs, inverse, top_rhs, top_blocks, *rest)
    smem = pl.BlockSpec(memory_space=pltpu.SMEM)
    results = pl.pallas_call(
        functools.partial(lower_kernel, sizes, order),
        out_shape=(
            jax.ShapeDtypeStruct((height, width), bf16),
            jax.ShapeDtypeStruct(rhs.shape, bf16),
            jax.ShapeDtypeStruct(top_rhs.shape, bf16),
        ),
        in_specs=[ANY, ANY, ANY, ANY, smem, *(ANY for _ in range(6))],
        out_specs=(ANY, ANY, ANY),
        scratch_shapes=[
            pltpu.VMEM((1, height), jnp.int32),
            *(pltpu.VMEM(array.shape, bf16) for array in held),
            pltpu.VMEM((height, height), bf16),
            pltpu.VMEM((height, height), bf16),
            pltpu.VMEM((2 * cols, devices, share, half), bf16),
            pltpu.VMEM((2 * cols, devices, share, half), bf16),
            pltpu.VMEM((devices, 1, 128), jnp.int32),
            pltpu.VMEM((devices, 1, 128), jnp.int32),
            pltpu.VMEM(blocks.shape, bf16),
            pltpu.VMEM((2 * cols, height, half), bf16),
            pltpu.VMEM((cols, rows, height, half), bf16),
            pltpu.VMEM((2, size, half), jnp.float32),
            pltpu.VMEM((cols, 2, size, half), bf16),
            pltpu.VMEM((2, cols, size, half), bf16),
            pltpu.VMEM((tops, 2 * pairs, depth, size), bf16),
            pltpu.VMEM((tops, 2, pairs, depth, size), bf16),
            pltpu.VMEM((tops, pairs, depth, size), bf16),
            pltpu.VMEM((tops, pairs, depth, size), bf16),
            pltpu.VMEM((tops, pairs, depth, size), bf16),
            pltpu.VMEM((tops, 2 * pairs, depth, size), bf16),
            pltpu.VMEM((height, width), bf16),
            pltpu.VMEM(rhs.shape, bf16),
            pltpu.VMEM(top_rhs.shape, bf16),
            dma((len(held) + 1,)),
            dma((2 * cols,)),
            dma((tops + 1,)),
            dma((2,)),
            dma((2,)),
            dma((2 * cols,)),
            dma((2 * cols,)),
            dma((cols,)),
            dma((cols, rows)),
            dma((2,)),
            dma((2,)),
            dma((tops,)),
            dma((tops,)),
            dma,
            dma((tops,)),
            dma,
            dma((tops, pairs)),
            dma,
            dma((tops,)),
        ],
        compiler_params=pltpu.CompilerParams(
            collective_id=1, has_side_effects=True, vmem_limit_bytes=60 * 2**20
        ),
        name="lower",
    )(
        target[None, :], rhs_in, leaf_inverse, blocks, pattern.T, rhs, inverse, top_rhs, top_blocks, *rest
    )
    return pl.pallas_call(
        hand_on,
        out_shape=tuple(jax.ShapeDtypeStruct(result.shape, bf16) for result in results),
        in_specs=[ANY, ANY, ANY],
        out_specs=(ANY, ANY, ANY),
        scratch_shapes=[
            *(pltpu.VMEM(result.shape, bf16) for result in results),
            dma((2, STRIPS + 2)),
        ],
        name="hand_on",
    )(*results)


def shards(
    rhs_in,
    rhs_target,
    leaf_inverse,
    level_one_blocks,
    level_one_pattern,
    level_one_rhs,
    level_one_inverse,
    top_blocks,
    top_rhs,
    top_inverse,
    top_chain,
):
    leaf_solution, solution_one, top_solution = all_levels(
        rhs_in,
        rhs_target,
        leaf_inverse,
        level_one_blocks[0, 0, 0],
        level_one_pattern[0, 0, 0],
        level_one_rhs[0, 0],
        level_one_inverse[0, 0],
        top_blocks[0, 0],
        top_rhs,
        top_inverse,
        top_chain,
    )
    return (leaf_solution, solution_one[None, None], top_solution)


def solution(mesh):
    in_specs = (
        P(("grid", "row", "col"), None),
        P(("grid", "row", "col")),
        P(("grid", "row", "col"), None, None),
        P("grid", "row", "col", None, None, None, None),
        P("grid", "row", "col", None, None),
        P("grid", "row", None, "col"),
        P("grid", "row", None, None),
        P("grid", "row", None, None, None),
        P(None, None, "col"),
        P(),
        P(),
    )
    out_specs = (
        P(("grid", "row", "col"), None),
        P("grid", "row", None, "col"),
        P(None, None, "col"),
    )
    return jax.shard_map(shards, mesh=mesh, in_specs=in_specs, out_specs=out_specs, check_vma=False)
```

```python
import functools

import jax
import jax.numpy as jnp
from jax import lax
from jax.experimental import pallas as pl
from jax.experimental.pallas import tpu as pltpu
from jax.sharding import PartitionSpec as P

MESH = pl.DeviceIdType.MESH
ANY = pl.BlockSpec(memory_space=pl.ANY)


def greet(axes, sizes):
    barrier = pltpu.get_barrier_semaphore()
    total = 1
    for size in sizes:
        total *= size
    flat = 0
    for axis, size in zip(axes, sizes):
        flat = flat * size + lax.axis_index(axis)

    @pl.loop(1, total)
    def _(step):
        rest = lax.rem(flat + step, total)
        coords = {}
        for axis, size in reversed(list(zip(axes, sizes))):
            coords[axis] = lax.rem(rest, size)
            rest = rest // size
        pl.semaphore_signal(barrier, inc=1, device_id=coords, device_id_type=MESH)

    return lambda: pl.semaphore_wait(barrier, total - 1)


def dot(a, b):
    return jnp.dot(a, b, preferred_element_type=jnp.float32)


def dot_t(a, b):
    return lax.dot_general(a, b, (((1,), (1,)), ((), ())), preferred_element_type=jnp.float32)


STRIPS = 8


def hand_on(leaf_in, one_in, top_in, leaf_out, one_out, top_out, leaf, one, top, sems):
    moves = []
    tall = leaf.shape[0] // STRIPS
    for strip in range(STRIPS):
        where = pl.ds(strip * tall, tall)
        moves.append((leaf_in.at[where], leaf.at[where], leaf_out.at[where]))
    moves += [(one_in, one, one_out), (top_in, top, top_out)]
    taken = [
        pltpu.make_async_copy(source, held, sems.at[0, at])
        for at, (source, held, _) in enumerate(moves)
    ]
    given = [
        pltpu.make_async_copy(held, into, sems.at[1, at])
        for at, (_, held, into) in enumerate(moves)
    ]
    for copy in taken:
        copy.start()
    for copy, after in zip(taken, given):
        copy.wait()
        after.start()
    for after in given:
        after.wait()


def lower_kernel(
    sizes,
    order,
    target_hbm,
    rhs_hbm,
    inverse_hbm,
    blocks_hbm,
    pattern_ref,
    rhs_one_hbm,
    inverse_one_hbm,
    top_rhs_hbm,
    top_blocks_hbm,
    top_inverse_hbm,
    chain_hbm,
    leaf_hbm,
    one_hbm,
    top_hbm,
    targets,
    rhs,
    inverse,
    own_blocks,
    rhs_one,
    inverse_one,
    top_rhs,
    top_blocks,
    top_inverse,
    chain,
    perm,
    fold,
    sorted_rows,
    got,
    places_out,
    got_places,
    other_blocks,
    solved,
    gathered,
    totals,
    pieces,
    landed,
    rhs_turned,
    terms,
    mate_terms,
    summed,
    sums,
    stacked,
    leaf,
    one,
    top_out,
    load_sems,
    leaf_sems,
    result_sems,
    block_sems,
    place_sems,
    row_send,
    row_recv,
    gather_send,
    gather_recv,
    piece_send,
    piece_recv,
    mate_send,
    mate_recv,
    sum_send,
    sum_recv,
    out_send,
    out_recv,
    on_send,
    on_recv,
):
    grids, rows, cols = sizes
    devices = grids * rows * cols
    row = lax.axis_index("row")
    col = lax.axis_index("col")
    me = (lax.axis_index("grid") * rows + row) * cols + col
    side = lax.rem(row, 2)
    mate = row + 1 - 2 * side
    leaves, size, _ = inverse.shape
    height = leaves * size
    chunk = leaf.shape[1] // cols
    half = chunk // 2
    share = got.shape[2]
    group = 128 // share

    units = 2 * cols
    ahead = 4
    met = greet(("grid", "row", "col"), sizes)
    loads = [
        pltpu.make_async_copy(source, into, load_sems.at[at])
        for at, (source, into) in enumerate(
            (
                (target_hbm, targets),
                (rhs_hbm, rhs),
                (inverse_hbm, inverse),
                (blocks_hbm, own_blocks),
                (rhs_one_hbm, rhs_one),
                (inverse_one_hbm, inverse_one),
                (top_rhs_hbm, top_rhs),
                (top_blocks_hbm, top_blocks),
                (top_inverse_hbm, top_inverse),
                (chain_hbm, chain),
            )
        )
    ]
    for load in loads:
        load.start()

    def column_of(part, which):
        pair = order[part // 2 * 2 : part // 2 * 2 + 2]
        return pair[which] if part % 2 == 0 else pair[1 - which]

    def columns(part, which):
        begin = column_of(part, which) * chunk + part % 2 * half
        return slice(begin, begin + half)

    def row_at(offset):
        pair = lax.rem(row // 2 + offset // 2, rows // 2)
        return pair * 2 + lax.rem(side + offset % 2, 2)

    def device_of(flat):
        return {
            "grid": flat // (rows * cols),
            "row": lax.rem(flat // cols, rows),
            "col": lax.rem(flat, cols),
        }

    def drain(ref, sem):
        pltpu.make_async_copy(ref, ref, sem).wait()

    def peer(step):
        return lax.rem(me + step, devices)

    def place_copy(step):
        target = peer(step)
        return pltpu.make_async_remote_copy(
            src_ref=places_out.at[target],
            dst_ref=got_places.at[me],
            send_sem=place_sems.at[0],
            recv_sem=place_sems.at[1],
            device_id=device_of(target),
            device_id_type=MESH,
        )

    def row_copy(unit, step):
        target = peer(step)
        return pltpu.make_async_remote_copy(
            src_ref=sorted_rows.at[unit, target],
            dst_ref=got.at[unit, me],
            send_sem=row_send.at[unit],
            recv_sem=row_recv.at[unit],
            device_id=device_of(target),
            device_id_type=MESH,
        )

    block_copy = pltpu.make_async_remote_copy(
        src_ref=own_blocks,
        dst_ref=other_blocks,
        send_sem=block_sems.at[0],
        recv_sem=block_sems.at[1],
        device_id={"row": mate},
        device_id_type=MESH,
    )

    def gather_copy(unit, target, owner):
        part = unit // 2
        return pltpu.make_async_remote_copy(
            src_ref=solved.at[unit],
            dst_ref=gathered.at[part, owner],
            send_sem=gather_send.at[part],
            recv_sem=gather_recv.at[part, owner],
            device_id={"row": target},
            device_id_type=MESH,
        )

    def piece_copy(part, which, into):
        return pltpu.make_async_remote_copy(
            src_ref=pieces.at[part, which],
            dst_ref=landed.at[part % 2, col],
            send_sem=piece_send.at[which],
            recv_sem=piece_recv.at[part % 2],
            device_id={"row": mate if which else row, "col": into},
            device_id_type=MESH,
        )

    span = height
    before = lax.broadcasted_iota(jnp.int32, (span, span), 0)
    after = lax.broadcasted_iota(jnp.int32, (span, span), 1)
    perm[...] = jnp.where(before < after, 1.0, 0.0).astype(perm.dtype)
    loads[0].wait()
    destination = targets[...] // height
    place = lax.rem(targets[...], height)
    for_device = lax.broadcasted_iota(jnp.int32, (devices, height), 0) == destination
    ones = jnp.where(for_device, 1.0, 0.0)
    counted = dot(ones.astype(perm.dtype), perm[...])
    rank = jnp.sum(ones * counted, axis=0, keepdims=True).astype(jnp.int32)
    slot = destination * share + rank

    lane = lax.broadcasted_iota(jnp.int32, (128, height), 0)
    to_lane = jnp.where(lane == lax.rem(me, group) * share + rank, 1.0, 0.0).astype(perm.dtype)
    high = (ones * (place // 32).astype(jnp.float32)).astype(perm.dtype)
    low = (ones * lax.rem(place, 32).astype(jnp.float32)).astype(perm.dtype)
    spread = dot_t(high, to_lane) * 32.0 + dot_t(low, to_lane)
    places_out[...] = spread.astype(jnp.int32).reshape(devices, 1, 128)
    got_places[me] = places_out[me]

    step_rows = 256
    for begin in range(0, height, step_rows):
        index = lax.broadcasted_iota(jnp.int32, (step_rows, height), 0) + begin
        perm[begin : begin + step_rows, :] = (
            jnp.where(index == slot, 1.0, 0.0).astype(perm.dtype)
        )
    loads[1].wait()

    def send_rows(unit):
        @pl.loop(1, devices)
        def _(step):
            row_copy(unit, step).start()

    for part in range(cols):
        taken = jnp.concatenate([rhs[:, columns(part, which)] for which in range(2)], axis=1)
        moved = dot(perm[...], taken).astype(got.dtype)
        for which in range(2):
            unit = 2 * part + which
            sorted_rows[unit] = moved[:, which * half : (which + 1) * half].reshape(
                devices, share, half
            )
            if unit == 0:
                met()

                @pl.loop(1, devices)
                def _(step):
                    place_copy(step).start()

            if unit < ahead:
                send_rows(unit)
            got[unit, me] = sorted_rows[unit, me]

    def masked(block, scale):
        return (block.astype(jnp.float32) * scale).astype(block.dtype)

    loads[3].wait()

    @pl.loop(0, rows)
    def _(owner):
        for leaf_at in range(leaves):
            own_blocks[owner, leaf_at] = masked(
                own_blocks[owner, leaf_at], pattern_ref[leaf_at, owner].astype(jnp.float32)
            )

    block_copy.start()
    loads[2].wait()
    drain(got_places.at[pl.ds(0, devices - 1)], place_sems.at[1])

    for block in range(height // 128):
        places = got_places[block * group]
        for other in range(1, group):
            places = places + got_places[block * group + other]
        index = lax.broadcasted_iota(jnp.int32, (height, 128), 0)
        perm[:, block * 128 : (block + 1) * 128] = jnp.where(index == places, 1.0, 0.0).astype(
            perm.dtype
        )
    for at in range(leaves):
        of_leaf = slice(at * size, (at + 1) * size)
        fold[of_leaf, :] = dot(inverse[at], perm[of_leaf, :]).astype(fold.dtype)

    for load in loads[4:]:
        load.wait()

    tops = top_blocks.shape[0]
    pairs = grids * rows // 2
    splits, depth = terms.shape[0], terms.shape[4]
    wide = chunk // splits
    for split in range(splits):
        for top in range(tops):
            part_rhs = top_rhs[top, :, split * wide : (split + 1) * wide]
            rhs_turned[split, top] = part_rhs.T.reshape(2 * pairs, depth, size)

    def leaf_copy(unit):
        where = columns(unit // 2, unit % 2)
        return pltpu.make_async_copy(leaf.at[:, where], leaf_hbm.at[:, where], leaf_sems.at[unit])

    def solve(unit):
        part, which = unit // 2, unit % 2
        drain(got.at[unit, pl.ds(0, devices - 1)], row_recv.at[unit])
        result = dot(fold[...], got[unit].reshape(height, half)).astype(leaf.dtype)
        solved[unit] = result
        for offset in range(1, rows // 2):
            target = lax.rem(row // 2 + offset, rows // 2) * 2 + which
            gather_copy(unit, target, row).start()

        @pl.when(side != which)
        def _():
            gather_copy(unit, mate, row).start()

        @pl.when(side == which)
        def _():
            gathered[part, row] = solved[unit]

        leaf[:, columns(part, which)] = result
        leaf_copy(unit).start()
        if unit + ahead < units:
            send_rows(unit + ahead)

    def add(part, owner):
        for which, blocks in enumerate((own_blocks, other_blocks)):
            term = dot(blocks[owner, 0], gathered[part, owner, :size])
            for at in range(1, leaves):
                term = term + dot(
                    blocks[owner, at], gathered[part, owner, at * size : (at + 1) * size]
                )
            totals[which] += term

    def couple(part):
        totals[...] = jnp.zeros_like(totals)

        @pl.loop(0, rows)
        def _(offset):
            owner = row_at(offset)

            @pl.when(offset > 0)
            def _():
                gather_copy(2 * part, owner, owner).wait_recv()

            add(part, owner)

        into = column_of(part, 0) + side * (column_of(part, 1) - column_of(part, 0))
        pieces[part] = totals[...].astype(pieces.dtype)
        piece_copy(part, 1, into).start()

        @pl.when(col != into)
        def _():
            piece_copy(part, 0, into).start()

        @pl.when(col == into)
        def _():
            landed[part % 2, col] = pieces[part, 0]

    for unit in range(units):
        solve(unit)
        if unit == 1:
            block_copy.wait()
        elif unit > 1 and unit % 2 == 0:
            couple(unit // 2 - 1)
    couple(cols - 1)

    second = 0
    for at in range(1, cols, 2):
        second = second + jnp.where(col == order[at], 1, 0)
    near = side + second - 2 * side * second

    def level_one(split):
        update = []
        for which in range(split * 2 // splits, (split + 1) * 2 // splits):

            @pl.when(near == which)
            def _(which=which):
                drain(landed.at[which, pl.ds(0, cols - 1)], piece_recv.at[which])

            @pl.when(near != which)
            def _(which=which):
                drain(landed.at[which], piece_recv.at[which])

            total = landed[which, 0].astype(jnp.float32)
            for source in range(1, cols):
                total = total + landed[which, source].astype(jnp.float32)
            update.append(total)
        where = slice(split * wide, (split + 1) * wide)
        resid = rhs_one[:, where].astype(jnp.float32) - jnp.concatenate(update, axis=1)
        solution = dot(inverse_one[...], resid.astype(jnp.bfloat16)).astype(one.dtype)
        one[:, where] = solution
        return solution

    pair = (lax.axis_index("grid") * rows + row) // 2
    here = 2 * pair + side

    def pair_at(step):
        return lax.rem(pair + step, pairs)

    def across(target):
        return {
            "grid": target // (rows // 2),
            "row": lax.rem(target, rows // 2) * 2 + side,
        }

    def mate_copy(split, top):
        return pltpu.make_async_remote_copy(
            src_ref=terms.at[split, top, 1 - side],
            dst_ref=mate_terms.at[split, top],
            send_sem=mate_send.at[split, top],
            recv_sem=mate_recv.at[split, top],
            device_id={"row": mate},
            device_id_type=MESH,
        )

    def sum_copy(split, top, target):
        return pltpu.make_async_remote_copy(
            src_ref=summed.at[split, top, target],
            dst_ref=sums.at[split, top, pair],
            send_sem=sum_send,
            recv_sem=sum_recv.at[split, top],
            device_id=across(target),
            device_id_type=MESH,
        )

    def out_copy(split, top, target, source):
        return pltpu.make_async_remote_copy(
            src_ref=stacked.at[split, top, here],
            dst_ref=stacked.at[split, top, 2 * source + side],
            send_sem=out_send,
            recv_sem=out_recv.at[split, top, source],
            device_id=across(target),
            device_id_type=MESH,
        )

    def on_copy(split, top, source):
        return pltpu.make_async_remote_copy(
            src_ref=stacked.at[split, top, 2 * source + side],
            dst_ref=stacked.at[split, top, 2 * source + side],
            send_sem=on_send,
            recv_sem=on_recv.at[split, top],
            device_id={"row": mate},
            device_id_type=MESH,
        )

    def spread_terms(split):
        turned = level_one(split).T
        for top in range(tops):
            term = dot_t(turned, top_blocks[top])
            for target in range(2 * pairs):
                terms[split, top, target % 2, target // 2] = term[
                    target * depth : (target + 1) * depth
                ].astype(terms.dtype)
            mate_copy(split, top).start()
        for top in range(tops):
            mate_copy(split, top).wait_recv()
            summed[split, top] = (
                terms[split, top, side].astype(jnp.float32)
                + mate_terms[split, top].astype(jnp.float32)
            ).astype(summed.dtype)
            for step in range(1, pairs):
                sum_copy(split, top, pair_at(step)).start()
            sums[split, top, pair] = summed[split, top, pair]

    def solve_tops(split):
        for top in range(tops):
            drain(sums.at[split, top, pl.ds(0, pairs - 1)], sum_recv.at[split, top])
            update = sums[split, top, 0].astype(jnp.float32)
            for other in range(1, pairs):
                update = update + sums[split, top, other].astype(jnp.float32)
            running = rhs_turned[split, top, here].astype(jnp.float32) - update
            for earlier in range(top):
                running = running - dot_t(
                    stacked[split, earlier, here], chain[top * (top - 1) // 2 + earlier]
                )
            stacked[split, top, here] = dot_t(
                running.astype(jnp.bfloat16), top_inverse[top]
            ).astype(stacked.dtype)
            for step in range(1, pairs):
                out_copy(split, top, pair_at(step), pair).start()
            on_copy(split, top, pair).start()

    def pass_on(split):
        for top in range(tops):
            for step in range(1, pairs):
                source = pair_at(step)
                out_copy(split, top, source, source).wait_recv()
                on_copy(split, top, source).start()

    def top_copy(split, top):
        where = slice(split * wide, (split + 1) * wide)
        return pltpu.make_async_copy(
            top_out.at[top, :, where], top_hbm.at[top, :, where], result_sems.at[split * tops + top]
        )

    def turn_back(split):
        for top in range(tops):
            drain(stacked.at[split, top, pl.ds(0, pairs)], on_recv.at[split, top])
            turned = stacked[split, top].reshape(2 * pairs * depth, size).T
            top_out[top, :, split * wide : (split + 1) * wide] = turned
            top_copy(split, top).start()

    for split in range(splits):
        spread_terms(split)
        if split + 1 == splits:
            one_copy = pltpu.make_async_copy(one, one_hbm, result_sems.at[splits * tops])
            one_copy.start()
        if split:
            pass_on(split - 1)
        solve_tops(split)
    for split in range(splits):
        if split + 1 == splits:
            pass_on(split)
        turn_back(split)

    drain(places_out.at[pl.ds(0, devices - 1)], place_sems.at[0])
    drain(pieces.at[:, 1], piece_send.at[1])

    for unit in range(units):
        drain(sorted_rows.at[unit, pl.ds(0, devices - 1)], row_send.at[unit])
        leaf_copy(unit).wait()
    for part in range(cols):
        drain(gathered.at[part, pl.ds(0, rows - 1)], gather_send.at[part])
    drain(pieces.at[pl.ds(0, cols - 1), 0], piece_send.at[0])
    for split in range(splits):
        for top in range(tops):
            mate_copy(split, top).wait_send()
            top_copy(split, top).wait()
    drain(summed.at[:, :, pl.ds(0, pairs - 1)], sum_send)
    drain(stacked.at[:, :, pl.ds(0, pairs - 1)], out_send)
    drain(stacked.at[:, :, pl.ds(0, pairs)], on_send)
    one_copy.wait()


def all_levels(rhs_in, target, leaf_inverse, blocks, pattern, rhs, inverse, top_blocks, top_rhs, *rest):
    sizes = tuple(lax.axis_size(axis) for axis in ("grid", "row", "col"))
    grids, rows, cols = sizes
    devices = grids * rows * cols
    height, width = rhs_in.shape
    share = height // devices
    owners, leaves, size, _ = blocks.shape
    chunk = width // cols
    half = chunk // 2
    bf16 = jnp.bfloat16
    order = sorted(range(cols), key=lambda part: -abs(2 * part - (cols - 1)))

    dma = pltpu.SemaphoreType.DMA
    tops = top_blocks.shape[0]
    pairs = grids * rows // 2
    depth = chunk // (2 * pairs)
    splits = 2 if depth % 32 == 0 else 1
    depth = depth // splits
    held = (rhs_in, leaf_inverse, blocks, rhs, inverse, top_rhs, top_blocks, *rest)
    smem = pl.BlockSpec(memory_space=pltpu.SMEM)
    results = pl.pallas_call(
        functools.partial(lower_kernel, sizes, order),
        out_shape=(
            jax.ShapeDtypeStruct((height, width), bf16),
            jax.ShapeDtypeStruct(rhs.shape, bf16),
            jax.ShapeDtypeStruct(top_rhs.shape, bf16),
        ),
        in_specs=[ANY, ANY, ANY, ANY, smem, *(ANY for _ in range(6))],
        out_specs=(ANY, ANY, ANY),
        scratch_shapes=[
            pltpu.VMEM((1, height), jnp.int32),
            *(pltpu.VMEM(array.shape, bf16) for array in held),
            pltpu.VMEM((height, height), bf16),
            pltpu.VMEM((height, height), bf16),
            pltpu.VMEM((2 * cols, devices, share, half), bf16),
            pltpu.VMEM((2 * cols, devices, share, half), bf16),
            pltpu.VMEM((devices, 1, 128), jnp.int32),
            pltpu.VMEM((devices, 1, 128), jnp.int32),
            pltpu.VMEM(blocks.shape, bf16),
            pltpu.VMEM((2 * cols, height, half), bf16),
            pltpu.VMEM((cols, rows, height, half), bf16),
            pltpu.VMEM((2, size, half), jnp.float32),
            pltpu.VMEM((cols, 2, size, half), bf16),
            pltpu.VMEM((2, cols, size, half), bf16),
            pltpu.VMEM((splits, tops, 2 * pairs, depth, size), bf16),
            pltpu.VMEM((splits, tops, 2, pairs, depth, size), bf16),
            pltpu.VMEM((splits, tops, pairs, depth, size), bf16),
            pltpu.VMEM((splits, tops, pairs, depth, size), bf16),
            pltpu.VMEM((splits, tops, pairs, depth, size), bf16),
            pltpu.VMEM((splits, tops, 2 * pairs, depth, size), bf16),
            pltpu.VMEM((height, width), bf16),
            pltpu.VMEM(rhs.shape, bf16),
            pltpu.VMEM(top_rhs.shape, bf16),
            dma((len(held) + 1,)),
            dma((2 * cols,)),
            dma((splits * tops + 1,)),
            dma((2,)),
            dma((2,)),
            dma((2 * cols,)),
            dma((2 * cols,)),
            dma((cols,)),
            dma((cols, rows)),
            dma((2,)),
            dma((2,)),
            dma((splits, tops)),
            dma((splits, tops)),
            dma,
            dma((splits, tops)),
            dma,
            dma((splits, tops, pairs)),
            dma,
            dma((splits, tops)),
        ],
        compiler_params=pltpu.CompilerParams(
            collective_id=1, has_side_effects=True, vmem_limit_bytes=60 * 2**20
        ),
        name="lower",
    )(
        target[None, :], rhs_in, leaf_inverse, blocks, pattern.T, rhs, inverse, top_rhs, top_blocks, *rest
    )
    return pl.pallas_call(
        hand_on,
        out_shape=tuple(jax.ShapeDtypeStruct(result.shape, bf16) for result in results),
        in_specs=[ANY, ANY, ANY],
        out_specs=(ANY, ANY, ANY),
        scratch_shapes=[
            *(pltpu.VMEM(result.shape, bf16) for result in results),
            dma((2, STRIPS + 2)),
        ],
        name="hand_on",
    )(*results)


def shards(
    rhs_in,
    rhs_target,
    leaf_inverse,
    level_one_blocks,
    level_one_pattern,
    level_one_rhs,
    level_one_inverse,
    top_blocks,
    top_rhs,
    top_inverse,
    top_chain,
):
    leaf_solution, solution_one, top_solution = all_levels(
        rhs_in,
        rhs_target,
        leaf_inverse,
        level_one_blocks[0, 0, 0],
        level_one_pattern[0, 0, 0],
        level_one_rhs[0, 0],
        level_one_inverse[0, 0],
        top_blocks[0, 0],
        top_rhs,
        top_inverse,
        top_chain,
    )
    return (leaf_solution, solution_one[None, None], top_solution)


def solution(mesh):
    in_specs = (
        P(("grid", "row", "col"), None),
        P(("grid", "row", "col")),
        P(("grid", "row", "col"), None, None),
        P("grid", "row", "col", None, None, None, None),
        P("grid", "row", "col", None, None),
        P("grid", "row", None, "col"),
        P("grid", "row", None, None),
        P("grid", "row", None, None, None),
        P(None, None, "col"),
        P(),
        P(),
    )
    out_specs = (
        P(("grid", "row", "col"), None),
        P("grid", "row", None, "col"),
        P(None, None, "col"),
    )
    return jax.shard_map(shards, mesh=mesh, in_specs=in_specs, out_specs=out_specs, check_vma=False)
```

```python
import functools

import jax
import jax.numpy as jnp
from jax import lax
from jax.experimental import pallas as pl
from jax.experimental.pallas import tpu as pltpu
from jax.sharding import PartitionSpec as P

MESH = pl.DeviceIdType.MESH
ANY = pl.BlockSpec(memory_space=pl.ANY)


def greet(axes, sizes):
    barrier = pltpu.get_barrier_semaphore()
    total = 1
    for size in sizes:
        total *= size
    flat = 0
    for axis, size in zip(axes, sizes):
        flat = flat * size + lax.axis_index(axis)

    @pl.loop(1, total)
    def _(step):
        rest = lax.rem(flat + step, total)
        coords = {}
        for axis, size in reversed(list(zip(axes, sizes))):
            coords[axis] = lax.rem(rest, size)
            rest = rest // size
        pl.semaphore_signal(barrier, inc=1, device_id=coords, device_id_type=MESH)

    return lambda: pl.semaphore_wait(barrier, total - 1)


def dot(a, b):
    return jnp.dot(a, b, preferred_element_type=jnp.float32)


def dot_t(a, b):
    return lax.dot_general(a, b, (((1,), (1,)), ((), ())), preferred_element_type=jnp.float32)


STRIPS = 8


def hand_on(leaf_in, one_in, top_in, leaf_out, one_out, top_out, leaf, one, top, sems):
    moves = []
    tall = leaf.shape[0] // STRIPS
    for strip in range(STRIPS):
        where = pl.ds(strip * tall, tall)
        moves.append((leaf_in.at[where], leaf.at[where], leaf_out.at[where]))
    moves += [(one_in, one, one_out), (top_in, top, top_out)]
    taken = [
        pltpu.make_async_copy(source, held, sems.at[0, at])
        for at, (source, held, _) in enumerate(moves)
    ]
    given = [
        pltpu.make_async_copy(held, into, sems.at[1, at])
        for at, (_, held, into) in enumerate(moves)
    ]
    for copy in taken:
        copy.start()
    for copy, after in zip(taken, given):
        copy.wait()
        after.start()
    for after in given:
        after.wait()


def lower_kernel(
    sizes,
    order,
    target_hbm,
    rhs_hbm,
    inverse_hbm,
    blocks_hbm,
    pattern_ref,
    rhs_one_hbm,
    inverse_one_hbm,
    top_rhs_hbm,
    top_blocks_hbm,
    top_inverse_hbm,
    chain_hbm,
    leaf_hbm,
    one_hbm,
    top_hbm,
    targets,
    rhs,
    inverse,
    own_blocks,
    rhs_one,
    inverse_one,
    top_rhs,
    top_blocks,
    top_inverse,
    chain,
    perm,
    fold,
    sorted_rows,
    got,
    places_out,
    got_places,
    other_blocks,
    solved,
    gathered,
    totals,
    pieces,
    landed,
    rhs_turned,
    terms,
    mate_terms,
    summed,
    sums,
    stacked,
    leaf,
    one,
    top_out,
    load_sems,
    leaf_sems,
    result_sems,
    block_sems,
    place_sems,
    row_send,
    row_recv,
    gather_send,
    gather_recv,
    piece_send,
    piece_recv,
    mate_send,
    mate_recv,
    sum_send,
    sum_recv,
    out_send,
    out_recv,
    on_send,
    on_recv,
):
    grids, rows, cols = sizes
    devices = grids * rows * cols
    row = lax.axis_index("row")
    col = lax.axis_index("col")
    me = (lax.axis_index("grid") * rows + row) * cols + col
    side = lax.rem(row, 2)
    mate = row + 1 - 2 * side
    leaves, size, _ = inverse.shape
    height = leaves * size
    chunk = leaf.shape[1] // cols
    half = chunk // 2
    share = got.shape[2]
    group = 128 // share

    units = 2 * cols
    ahead = 2
    met = greet(("grid", "row", "col"), sizes)
    loads = [
        pltpu.make_async_copy(source, into, load_sems.at[at])
        for at, (source, into) in enumerate(
            (
                (target_hbm, targets),
                (rhs_hbm, rhs),
                (inverse_hbm, inverse),
                (blocks_hbm, own_blocks),
                (rhs_one_hbm, rhs_one),
                (inverse_one_hbm, inverse_one),
                (top_rhs_hbm, top_rhs),
                (top_blocks_hbm, top_blocks),
                (top_inverse_hbm, top_inverse),
                (chain_hbm, chain),
            )
        )
    ]
    for load in loads:
        load.start()

    def column_of(part, which):
        pair = order[part // 2 * 2 : part // 2 * 2 + 2]
        return pair[which] if part % 2 == 0 else pair[1 - which]

    def columns(part, which):
        begin = column_of(part, which) * chunk + part % 2 * half
        return slice(begin, begin + half)

    def row_at(offset):
        pair = lax.rem(row // 2 + offset // 2, rows // 2)
        return pair * 2 + lax.rem(side + offset % 2, 2)

    def device_of(flat):
        return {
            "grid": flat // (rows * cols),
            "row": lax.rem(flat // cols, rows),
            "col": lax.rem(flat, cols),
        }

    def drain(ref, sem):
        pltpu.make_async_copy(ref, ref, sem).wait()

    def peer(step):
        return lax.rem(me + step, devices)

    def place_copy(step):
        target = peer(step)
        return pltpu.make_async_remote_copy(
            src_ref=places_out.at[target],
            dst_ref=got_places.at[me],
            send_sem=place_sems.at[0],
            recv_sem=place_sems.at[1],
            device_id=device_of(target),
            device_id_type=MESH,
        )

    def row_copy(part, step):
        target = peer(step)
        return pltpu.make_async_remote_copy(
            src_ref=sorted_rows.at[part, target],
            dst_ref=got.at[part, me],
            send_sem=row_send.at[part],
            recv_sem=row_recv.at[part],
            device_id=device_of(target),
            device_id_type=MESH,
        )

    block_copy = pltpu.make_async_remote_copy(
        src_ref=own_blocks,
        dst_ref=other_blocks,
        send_sem=block_sems.at[0],
        recv_sem=block_sems.at[1],
        device_id={"row": mate},
        device_id_type=MESH,
    )

    def gather_copy(unit, target, owner):
        part = unit // 2
        return pltpu.make_async_remote_copy(
            src_ref=solved.at[unit],
            dst_ref=gathered.at[part, owner],
            send_sem=gather_send.at[part],
            recv_sem=gather_recv.at[part, owner],
            device_id={"row": target},
            device_id_type=MESH,
        )

    def piece_copy(part, which, into):
        return pltpu.make_async_remote_copy(
            src_ref=pieces.at[part, which],
            dst_ref=landed.at[part % 2, col],
            send_sem=piece_send.at[which],
            recv_sem=piece_recv.at[part % 2],
            device_id={"row": mate if which else row, "col": into},
            device_id_type=MESH,
        )

    span = height
    before = lax.broadcasted_iota(jnp.int32, (span, span), 0)
    after = lax.broadcasted_iota(jnp.int32, (span, span), 1)
    perm[...] = jnp.where(before < after, 1.0, 0.0).astype(perm.dtype)
    loads[0].wait()
    destination = targets[...] // height
    place = lax.rem(targets[...], height)
    for_device = lax.broadcasted_iota(jnp.int32, (devices, height), 0) == destination
    ones = jnp.where(for_device, 1.0, 0.0)
    counted = dot(ones.astype(perm.dtype), perm[...])
    rank = jnp.sum(ones * counted, axis=0, keepdims=True).astype(jnp.int32)
    slot = destination * share + rank

    lane = lax.broadcasted_iota(jnp.int32, (128, height), 0)
    to_lane = jnp.where(lane == lax.rem(me, group) * share + rank, 1.0, 0.0).astype(perm.dtype)
    high = (ones * (place // 32).astype(jnp.float32)).astype(perm.dtype)
    low = (ones * lax.rem(place, 32).astype(jnp.float32)).astype(perm.dtype)
    spread = dot_t(high, to_lane) * 32.0 + dot_t(low, to_lane)
    places_out[...] = spread.astype(jnp.int32).reshape(devices, 1, 128)
    got_places[me] = places_out[me]

    step_rows = 256
    for begin in range(0, height, step_rows):
        index = lax.broadcasted_iota(jnp.int32, (step_rows, height), 0) + begin
        perm[begin : begin + step_rows, :] = (
            jnp.where(index == slot, 1.0, 0.0).astype(perm.dtype)
        )
    loads[1].wait()

    def send_rows(part):
        @pl.loop(1, devices)
        def _(step):
            row_copy(part, step).start()

    for part in range(cols):
        taken = jnp.concatenate([rhs[:, columns(part, which)] for which in range(2)], axis=1)
        moved = dot(perm[...], taken).astype(got.dtype)
        sorted_rows[part] = moved.reshape(devices, share, chunk)
        if part == 0:
            met()

            @pl.loop(1, devices)
            def _(step):
                place_copy(step).start()

        if part < ahead:
            send_rows(part)
        got[part, me] = sorted_rows[part, me]

    def masked(block, scale):
        return (block.astype(jnp.float32) * scale).astype(block.dtype)

    loads[3].wait()

    @pl.loop(0, rows)
    def _(owner):
        for leaf_at in range(leaves):
            own_blocks[owner, leaf_at] = masked(
                own_blocks[owner, leaf_at], pattern_ref[leaf_at, owner].astype(jnp.float32)
            )

    block_copy.start()
    loads[2].wait()
    drain(got_places.at[pl.ds(0, devices - 1)], place_sems.at[1])

    for block in range(height // 128):
        places = got_places[block * group]
        for other in range(1, group):
            places = places + got_places[block * group + other]
        index = lax.broadcasted_iota(jnp.int32, (height, 128), 0)
        perm[:, block * 128 : (block + 1) * 128] = jnp.where(index == places, 1.0, 0.0).astype(
            perm.dtype
        )
    for at in range(leaves):
        of_leaf = slice(at * size, (at + 1) * size)
        fold[of_leaf, :] = dot(inverse[at], perm[of_leaf, :]).astype(fold.dtype)

    for load in loads[4:]:
        load.wait()

    tops = top_blocks.shape[0]
    pairs = grids * rows // 2
    splits, depth = terms.shape[0], terms.shape[4]
    wide = chunk // splits
    for split in range(splits):
        for top in range(tops):
            part_rhs = top_rhs[top, :, split * wide : (split + 1) * wide]
            rhs_turned[split, top] = part_rhs.T.reshape(2 * pairs, depth, size)

    def leaf_copy(unit):
        where = columns(unit // 2, unit % 2)
        return pltpu.make_async_copy(leaf.at[:, where], leaf_hbm.at[:, where], leaf_sems.at[unit])

    def solve(part):
        drain(got.at[part, pl.ds(0, devices - 1)], row_recv.at[part])
        result = dot(fold[...], got[part].reshape(height, chunk)).astype(leaf.dtype)
        for which in range(2):
            unit = 2 * part + which
            solved[unit] = result[:, which * half : (which + 1) * half]
            for offset in range(1, rows // 2):
                target = lax.rem(row // 2 + offset, rows // 2) * 2 + which
                gather_copy(unit, target, row).start()

            @pl.when(side != which)
            def _(unit=unit):
                gather_copy(unit, mate, row).start()

        gathered[part, row] = solved[2 * part + side]
        if part + ahead < cols:
            send_rows(part + ahead)
        for which in range(2):
            leaf[:, columns(part, which)] = result[:, which * half : (which + 1) * half]
            leaf_copy(2 * part + which).start()

    def add(part, owner):
        for which, blocks in enumerate((own_blocks, other_blocks)):
            term = dot(blocks[owner, 0], gathered[part, owner, :size])
            for at in range(1, leaves):
                term = term + dot(
                    blocks[owner, at], gathered[part, owner, at * size : (at + 1) * size]
                )
            totals[which] += term

    def couple(part):
        totals[...] = jnp.zeros_like(totals)

        @pl.loop(0, rows)
        def _(offset):
            owner = row_at(offset)

            @pl.when(offset > 0)
            def _():
                gather_copy(2 * part, owner, owner).wait_recv()

            add(part, owner)

        into = column_of(part, 0) + side * (column_of(part, 1) - column_of(part, 0))
        pieces[part] = totals[...].astype(pieces.dtype)
        piece_copy(part, 1, into).start()

        @pl.when(col != into)
        def _():
            piece_copy(part, 0, into).start()

        @pl.when(col == into)
        def _():
            landed[part % 2, col] = pieces[part, 0]

    for part in range(cols):
        solve(part)
        if part == 0:
            block_copy.wait()
        else:
            couple(part - 1)
    couple(cols - 1)

    second = 0
    for at in range(1, cols, 2):
        second = second + jnp.where(col == order[at], 1, 0)
    near = side + second - 2 * side * second

    def level_one(split):
        update = []
        for which in range(split * 2 // splits, (split + 1) * 2 // splits):

            @pl.when(near == which)
            def _(which=which):
                drain(landed.at[which, pl.ds(0, cols - 1)], piece_recv.at[which])

            @pl.when(near != which)
            def _(which=which):
                drain(landed.at[which], piece_recv.at[which])

            total = landed[which, 0].astype(jnp.float32)
            for source in range(1, cols):
                total = total + landed[which, source].astype(jnp.float32)
            update.append(total)
        where = slice(split * wide, (split + 1) * wide)
        resid = rhs_one[:, where].astype(jnp.float32) - jnp.concatenate(update, axis=1)
        solution = dot(inverse_one[...], resid.astype(jnp.bfloat16)).astype(one.dtype)
        one[:, where] = solution
        return solution

    pair = (lax.axis_index("grid") * rows + row) // 2
    here = 2 * pair + side

    def pair_at(step):
        return lax.rem(pair + step, pairs)

    def across(target):
        return {
            "grid": target // (rows // 2),
            "row": lax.rem(target, rows // 2) * 2 + side,
        }

    def mate_copy(split, top):
        return pltpu.make_async_remote_copy(
            src_ref=terms.at[split, top, 1 - side],
            dst_ref=mate_terms.at[split, top],
            send_sem=mate_send.at[split, top],
            recv_sem=mate_recv.at[split, top],
            device_id={"row": mate},
            device_id_type=MESH,
        )

    def sum_copy(split, top, target):
        return pltpu.make_async_remote_copy(
            src_ref=summed.at[split, top, target],
            dst_ref=sums.at[split, top, pair],
            send_sem=sum_send,
            recv_sem=sum_recv.at[split, top],
            device_id=across(target),
            device_id_type=MESH,
        )

    def out_copy(split, top, target, source):
        return pltpu.make_async_remote_copy(
            src_ref=stacked.at[split, top, here],
            dst_ref=stacked.at[split, top, 2 * source + side],
            send_sem=out_send,
            recv_sem=out_recv.at[split, top, source],
            device_id=across(target),
            device_id_type=MESH,
        )

    def on_copy(split, top, source):
        return pltpu.make_async_remote_copy(
            src_ref=stacked.at[split, top, 2 * source + side],
            dst_ref=stacked.at[split, top, 2 * source + side],
            send_sem=on_send,
            recv_sem=on_recv.at[split, top],
            device_id={"row": mate},
            device_id_type=MESH,
        )

    def spread_terms(split):
        turned = level_one(split).T
        for top in range(tops):
            term = dot_t(turned, top_blocks[top])
            for target in range(2 * pairs):
                terms[split, top, target % 2, target // 2] = term[
                    target * depth : (target + 1) * depth
                ].astype(terms.dtype)
            mate_copy(split, top).start()
        for top in range(tops):
            mate_copy(split, top).wait_recv()
            summed[split, top] = (
                terms[split, top, side].astype(jnp.float32)
                + mate_terms[split, top].astype(jnp.float32)
            ).astype(summed.dtype)
            for step in range(1, pairs):
                sum_copy(split, top, pair_at(step)).start()
            sums[split, top, pair] = summed[split, top, pair]

    def solve_tops(split):
        for top in range(tops):
            drain(sums.at[split, top, pl.ds(0, pairs - 1)], sum_recv.at[split, top])
            update = sums[split, top, 0].astype(jnp.float32)
            for other in range(1, pairs):
                update = update + sums[split, top, other].astype(jnp.float32)
            running = rhs_turned[split, top, here].astype(jnp.float32) - update
            for earlier in range(top):
                running = running - dot_t(
                    stacked[split, earlier, here], chain[top * (top - 1) // 2 + earlier]
                )
            stacked[split, top, here] = dot_t(
                running.astype(jnp.bfloat16), top_inverse[top]
            ).astype(stacked.dtype)
            for step in range(1, pairs):
                out_copy(split, top, pair_at(step), pair).start()
            on_copy(split, top, pair).start()

    def pass_on(split, top):
        for step in range(1, pairs):
            source = pair_at(step)
            out_copy(split, top, source, source).wait_recv()
            on_copy(split, top, source).start()

    def top_copy(split, top):
        where = slice(split * wide, (split + 1) * wide)
        return pltpu.make_async_copy(
            top_out.at[top, :, where], top_hbm.at[top, :, where], result_sems.at[split * tops + top]
        )

    def turn_back(split, top):
        drain(stacked.at[split, top, pl.ds(0, pairs)], on_recv.at[split, top])
        turned = stacked[split, top].reshape(2 * pairs * depth, size).T
        top_out[top, :, split * wide : (split + 1) * wide] = turned
        top_copy(split, top).start()

    for split in range(splits):
        spread_terms(split)
        if split + 1 == splits:
            one_copy = pltpu.make_async_copy(one, one_hbm, result_sems.at[splits * tops])
            one_copy.start()
        if split:
            for top in range(tops):
                pass_on(split - 1, top)
        solve_tops(split)
    for split in range(splits - 1):
        for top in range(tops):
            turn_back(split, top)
    behind = min(2, tops)
    for top in range(tops):
        pass_on(splits - 1, top)
        if top >= behind:
            turn_back(splits - 1, top - behind)
    for top in range(tops - behind, tops):
        turn_back(splits - 1, top)

    drain(places_out.at[pl.ds(0, devices - 1)], place_sems.at[0])
    drain(pieces.at[:, 1], piece_send.at[1])

    for unit in range(units):
        leaf_copy(unit).wait()
    for part in range(cols):
        drain(sorted_rows.at[part, pl.ds(0, devices - 1)], row_send.at[part])
        drain(gathered.at[part, pl.ds(0, rows - 1)], gather_send.at[part])
    drain(pieces.at[pl.ds(0, cols - 1), 0], piece_send.at[0])
    for split in range(splits):
        for top in range(tops):
            mate_copy(split, top).wait_send()
            top_copy(split, top).wait()
    drain(summed.at[:, :, pl.ds(0, pairs - 1)], sum_send)
    drain(stacked.at[:, :, pl.ds(0, pairs - 1)], out_send)
    drain(stacked.at[:, :, pl.ds(0, pairs)], on_send)
    one_copy.wait()


def all_levels(rhs_in, target, leaf_inverse, blocks, pattern, rhs, inverse, top_blocks, top_rhs, *rest):
    sizes = tuple(lax.axis_size(axis) for axis in ("grid", "row", "col"))
    grids, rows, cols = sizes
    devices = grids * rows * cols
    height, width = rhs_in.shape
    share = height // devices
    owners, leaves, size, _ = blocks.shape
    chunk = width // cols
    half = chunk // 2
    bf16 = jnp.bfloat16
    order = sorted(range(cols), key=lambda part: -abs(2 * part - (cols - 1)))

    dma = pltpu.SemaphoreType.DMA
    tops = top_blocks.shape[0]
    pairs = grids * rows // 2
    depth = chunk // (2 * pairs)
    splits = 2 if depth % 32 == 0 else 1
    depth = depth // splits
    held = (rhs_in, leaf_inverse, blocks, rhs, inverse, top_rhs, top_blocks, *rest)
    smem = pl.BlockSpec(memory_space=pltpu.SMEM)
    results = pl.pallas_call(
        functools.partial(lower_kernel, sizes, order),
        out_shape=(
            jax.ShapeDtypeStruct((height, width), bf16),
            jax.ShapeDtypeStruct(rhs.shape, bf16),
            jax.ShapeDtypeStruct(top_rhs.shape, bf16),
        ),
        in_specs=[ANY, ANY, ANY, ANY, smem, *(ANY for _ in range(6))],
        out_specs=(ANY, ANY, ANY),
        scratch_shapes=[
            pltpu.VMEM((1, height), jnp.int32),
            *(pltpu.VMEM(array.shape, bf16) for array in held),
            pltpu.VMEM((height, height), bf16),
            pltpu.VMEM((height, height), bf16),
            pltpu.VMEM((cols, devices, share, chunk), bf16),
            pltpu.VMEM((cols, devices, share, chunk), bf16),
            pltpu.VMEM((devices, 1, 128), jnp.int32),
            pltpu.VMEM((devices, 1, 128), jnp.int32),
            pltpu.VMEM(blocks.shape, bf16),
            pltpu.VMEM((2 * cols, height, half), bf16),
            pltpu.VMEM((cols, rows, height, half), bf16),
            pltpu.VMEM((2, size, half), jnp.float32),
            pltpu.VMEM((cols, 2, size, half), bf16),
            pltpu.VMEM((2, cols, size, half), bf16),
            pltpu.VMEM((splits, tops, 2 * pairs, depth, size), bf16),
            pltpu.VMEM((splits, tops, 2, pairs, depth, size), bf16),
            pltpu.VMEM((splits, tops, pairs, depth, size), bf16),
            pltpu.VMEM((splits, tops, pairs, depth, size), bf16),
            pltpu.VMEM((splits, tops, pairs, depth, size), bf16),
            pltpu.VMEM((splits, tops, 2 * pairs, depth, size), bf16),
            pltpu.VMEM((height, width), bf16),
            pltpu.VMEM(rhs.shape, bf16),
            pltpu.VMEM(top_rhs.shape, bf16),
            dma((len(held) + 1,)),
            dma((2 * cols,)),
            dma((splits * tops + 1,)),
            dma((2,)),
            dma((2,)),
            dma((cols,)),
            dma((cols,)),
            dma((cols,)),
            dma((cols, rows)),
            dma((2,)),
            dma((2,)),
            dma((splits, tops)),
            dma((splits, tops)),
            dma,
            dma((splits, tops)),
            dma,
            dma((splits, tops, pairs)),
            dma,
            dma((splits, tops)),
        ],
        compiler_params=pltpu.CompilerParams(
            collective_id=1, has_side_effects=True, vmem_limit_bytes=60 * 2**20
        ),
        name="lower",
    )(
        target[None, :], rhs_in, leaf_inverse, blocks, pattern.T, rhs, inverse, top_rhs, top_blocks, *rest
    )
    return pl.pallas_call(
        hand_on,
        out_shape=tuple(jax.ShapeDtypeStruct(result.shape, bf16) for result in results),
        in_specs=[ANY, ANY, ANY],
        out_specs=(ANY, ANY, ANY),
        scratch_shapes=[
            *(pltpu.VMEM(result.shape, bf16) for result in results),
            dma((2, STRIPS + 2)),
        ],
        name="hand_on",
    )(*results)


def shards(
    rhs_in,
    rhs_target,
    leaf_inverse,
    level_one_blocks,
    level_one_pattern,
    level_one_rhs,
    level_one_inverse,
    top_blocks,
    top_rhs,
    top_inverse,
    top_chain,
):
    leaf_solution, solution_one, top_solution = all_levels(
        rhs_in,
        rhs_target,
        leaf_inverse,
        level_one_blocks[0, 0, 0],
        level_one_pattern[0, 0, 0],
        level_one_rhs[0, 0],
        level_one_inverse[0, 0],
        top_blocks[0, 0],
        top_rhs,
        top_inverse,
        top_chain,
    )
    return (leaf_solution, solution_one[None, None], top_solution)


def solution(mesh):
    in_specs = (
        P(("grid", "row", "col"), None),
        P(("grid", "row", "col")),
        P(("grid", "row", "col"), None, None),
        P("grid", "row", "col", None, None, None, None),
        P("grid", "row", "col", None, None),
        P("grid", "row", None, "col"),
        P("grid", "row", None, None),
        P("grid", "row", None, None, None),
        P(None, None, "col"),
        P(),
        P(),
    )
    out_specs = (
        P(("grid", "row", "col"), None),
        P("grid", "row", None, "col"),
        P(None, None, "col"),
    )
    return jax.shard_map(shards, mesh=mesh, in_specs=in_specs, out_specs=out_specs, check_vma=False)
```
